256 devices in a mesh: group: 2 (over z_lo), dp: 16 (over y, z_hi), mp: 8 (over x, core).
Axes of the slice: x: 4, y: 4, z: 8 (z_hi: 4, z_lo: 2; z = z_hi * 2 + z_lo), core: 2. Of those that a mesh axis runs over, the one named last changes fastest.
Arguments:
- teacher_hidden: bfloat16 [2048, 8192], P('dp', ('group', 'mp')), may hold values from -6 to 6
- teacher_gain: bfloat16 [8192], P(('group', 'mp')), may hold values from 0.25 to 1.75
- teacher_head: bfloat16 [8192, 8192], P(('group', 'mp')), may hold values from -0.198873782 to 0.198873782
- student_hidden: bfloat16 [2048, 4096], P('dp'), may hold values from -6 to 6
- student_head: bfloat16 [4096, 8192], P('dp', ('group', 'mp')), may hold values from -0.28125 to 0.28125
- depth_cut: int32 [32], P('dp'), may hold values from 1 to 4
Outputs:
- kl_terms: float32 [4, 2048], P(None, 'dp')
- hidden_grad: float32 [2048, 4096], P('dp', ('group', 'mp'))
- head_grad: float32 [4096, 8192], P('dp', ('group', 'mp'))
The draws below stay inside these ranges and needn't reach their ends.
Inputs may be any that keep to these rules, and one draw needn't show every extreme that they name: `depth_cut`: each sample's number of codebooks kept.
All inputs are finite; a program needn't handle non-finite values.
Results may differ from the reference program's by a relative error of at most 0.0053.
Values may be sent and summed in bfloat16 or wider, within the bound.
No kernel may reach another device: no remote copies, remote signals or barrier semaphores. Data moves between devices by JAX's collectives and lax.ppermute only.
A program may use at most 128 MiB of HBM per device.

```python
import jax
import jax.numpy as jnp
from jax import lax

DT = 8192
DS = 4096
C = 4
V = 2048
FRAMES = 64
TOKENS = 2048
SAMPLES = 32


def drawn_rows(key, salt_code, feature_count):
    noise_key = jax.random.fold_in(key, salt_code)
    return jnp.clip(jax.random.normal(noise_key, (TOKENS, feature_count), jnp.float32), -6.0, 6.0)


def drawn_head(key, salt_code, feature_count):
    noise_key = jax.random.fold_in(key, salt_code)
    normal_values = jnp.clip(jax.random.normal(noise_key, (feature_count, C * V), jnp.float32), -6.0, 6.0)
    return normal_values * (3.0 * feature_count ** (-0.5))


def draw_teacher_hidden(key, part):
    values = drawn_rows(key, 101, DT)
    return values.astype(jnp.bfloat16)


def draw_student_hidden(key, part):
    values = drawn_rows(key, 103, DS)
    return values.astype(jnp.bfloat16)


def draw_teacher_head(key, part):
    values = drawn_head(key, 102, DT)
    return values.astype(jnp.bfloat16)


def draw_student_head(key, part):
    values = drawn_head(key, 104, DS)
    return values.astype(jnp.bfloat16)


def place_ends(values, rng, low, largest):
    longest = values.shape.index(max(values.shape))
    spots = []
    for shift in (0, 1):
        where = [jax.random.randint(jax.random.fold_in(rng, axis), (), 0, length) for axis, length in enumerate(values.shape)]
        where[longest] = (where[longest] + shift) % values.shape[longest]
        spots.append(tuple(where))
    return values.at[spots[0]].set(low).at[spots[1]].set(largest)


def setup_inputs(seed: int = 0) -> dict:
    seeds = jax.random.split(jax.random.key(seed), 7)
    return {
        "teacher_hidden": draw_teacher_hidden(jax.random.fold_in(seeds[6], 71), 0),
        "teacher_gain": jnp.clip(1.0 + 0.15 * jax.random.normal(seeds[1], (DT,), jnp.float32), 0.25, 1.75).astype(jnp.bfloat16),
        "teacher_head": draw_teacher_head(jax.random.fold_in(seeds[6], 71), 0),
        "student_hidden": draw_student_hidden(jax.random.fold_in(seeds[6], 71), 0),
        "student_head": draw_student_head(jax.random.fold_in(seeds[6], 71), 0),
        "depth_cut": place_ends(jax.random.randint(seeds[5], (SAMPLES,), 1, C + 1), jax.random.fold_in(seeds[5], 1), 1, C).astype(jnp.int32),
    }


epsilon = 1e-05

def reference(teacher_hidden, teacher_gain, teacher_head, student_hidden, student_head, depth_cut):
    hidden_float = teacher_hidden.astype(jnp.float32)
    squares = lax.optimization_barrier(jnp.mean(hidden_float * hidden_float, axis=1, keepdims=True))
    normed = (hidden_float * lax.rsqrt(squares + epsilon) * teacher_gain.astype(jnp.float32)[None, :]).astype(jnp.bfloat16)
    teacher_scores = jnp.dot(normed, teacher_head, preferred_element_type=jnp.float32).reshape(TOKENS, C, V)
    student_scores = jnp.dot(student_hidden, student_head, preferred_element_type=jnp.float32).reshape(TOKENS, C, V)
    teacher_log = jax.nn.log_softmax(teacher_scores, axis=2)
    student_log = jax.nn.log_softmax(student_scores, axis=2)
    teacher_prob = jnp.exp(teacher_log)
    divergence = lax.optimization_barrier(jnp.sum(teacher_prob * (teacher_log - student_log), axis=2))
    depth_rows = jnp.repeat(depth_cut, FRAMES)
    alive_mask = (jnp.arange(C, dtype=jnp.int32)[None, :] < depth_rows[:, None]).astype(jnp.float32)
    depth_weight = alive_mask / depth_rows[:, None].astype(jnp.float32)
    kl_terms = (divergence * depth_weight).T
    score_grad = ((jnp.exp(student_log) - teacher_prob) * depth_weight[:, :, None]).reshape(TOKENS, C * V).astype(jnp.bfloat16)
    hidden_grad = jnp.dot(score_grad, student_head.T, preferred_element_type=jnp.float32)
    head_grad = jnp.dot(student_hidden.T, score_grad, preferred_element_type=jnp.float32)
    return (kl_terms, hidden_grad, head_grad)
```

```python
import jax
import jax.numpy as jnp
from jax import lax
from jax.experimental import pallas as pl
from jax.experimental.pallas import tpu as pltpu
from jax.sharding import PartitionSpec as P

DT = 8192
C = 4
FRAMES = 64
epsilon = 1e-05

ALL = ("group", "dp", "mp")
PLANE = ("group", "mp")


def place(zl, y, zh, x, core):
    return zl * 128 + (y % 4 * 4 + zh % 4) * 8 + x % 4 * 2 + core


def send(value, target):
    pairs = []
    for zl in range(2):
        for y in range(4):
            for zh in range(4):
                for x in range(4):
                    for core in range(2):
                        pairs.append((place(zl, y, zh, x, core), place(*target(zl, y, zh, x, core))))
    return lax.ppermute(value, ALL, pairs)


def to_y(value, step):
    return send(value, lambda zl, y, zh, x, core: (zl, y + step, zh, x, core))


def to_zh(value, step):
    return send(value, lambda zl, y, zh, x, core: (zl, y, zh + step, x, core))


def to_x(value, step):
    return send(value, lambda zl, y, zh, x, core: (zl, y, zh, x + step, core))


def to_zl(value):
    return send(value, lambda zl, y, zh, x, core: (1 - zl, y, zh, x, core))


def to_core(value):
    return send(value, lambda zl, y, zh, x, core: (zl, y, zh, x, 1 - core))


def pick_kernel(order_ref, hidden_ref, out_ref):
    out_ref[0] = hidden_ref[...]


def picked_blocks(hidden, order):
    rows = hidden.shape[0]
    count = order.shape[0]
    return pl.pallas_call(
        pick_kernel,
        grid_spec=pltpu.PrefetchScalarGridSpec(
            num_scalar_prefetch=1,
            grid=(count,),
            in_specs=[pl.BlockSpec((rows, 256), lambda i, order_ref: (0, order_ref[i]))],
            out_specs=pl.BlockSpec((1, rows, 256), lambda i, order_ref: (i, 0, 0)),
        ),
        out_shape=jax.ShapeDtypeStruct((count, rows, 256), hidden.dtype),
        name="pick",
    )(order, hidden)


def teacher_kernel(order_ref, normed_ref, head_ref, out_ref):
    out_ref[0] = jnp.dot(normed_ref[...], head_ref[...], preferred_element_type=jnp.float32)


def teacher_parts(normed, head, order):
    rows, depth = normed.shape
    count = order.shape[0]
    return pl.pallas_call(
        teacher_kernel,
        grid_spec=pltpu.PrefetchScalarGridSpec(
            num_scalar_prefetch=1,
            grid=(count,),
            in_specs=[
                pl.BlockSpec((rows, depth), lambda i, order_ref: (0, 0)),
                pl.BlockSpec((depth, 512), lambda i, order_ref: (0, order_ref[i])),
            ],
            out_specs=pl.BlockSpec((1, rows, 512), lambda i, order_ref: (i, 0, 0)),
        ),
        out_shape=jax.ShapeDtypeStruct((count, rows, 512), jnp.float32),
        name="teacher",
    )(order, normed, head)


def student_kernel(*refs):
    hidden_refs, head_refs, out_ref = refs[:4], refs[4:8], refs[8]
    for k in range(4):
        total = None
        for j in range(4):
            term = jnp.dot(hidden_refs[k][j], head_refs[j][...], preferred_element_type=jnp.float32)
            total = term if total is None else total + term
        out_ref[k] = total


def student_parts(hidden_slots, head_slots):
    return pl.pallas_call(
        student_kernel,
        out_shape=jax.ShapeDtypeStruct((4, 128, 512), jnp.float32),
        name="student",
    )(*hidden_slots, *head_slots)


def head_grad_kernel(*refs):
    hidden_refs, grad_refs, own_ref, out_ref = refs[:4], refs[4:8], refs[8], refs[9]
    for j in range(4):
        total = None
        for k in range(4):
            term = lax.dot_general(
                hidden_refs[k][j], grad_refs[k][...], (((0,), (0,)), ((), ())), preferred_element_type=jnp.float32
            )
            total = term if total is None else total + term
        if j == 0:
            own_ref[...] = total
        else:
            out_ref[j - 1] = total.astype(out_ref.dtype)


def head_grad_parts(hidden_slots, grad_slots):
    return pl.pallas_call(
        head_grad_kernel,
        out_shape=(
            jax.ShapeDtypeStruct((256, 512), jnp.float32),
            jax.ShapeDtypeStruct((3, 256, 512), jnp.bfloat16),
        ),
        name="head_grad",
    )(*hidden_slots, *grad_slots)


def hidden_grad_kernel(*refs):
    grad_refs, head_refs, out_ref = refs[:4], refs[4:8], refs[8]
    for k in range(4):
        for j in range(4):
            out_ref[4 * k + j] = lax.dot_general(
                grad_refs[k][...], head_refs[j][...], (((1,), (1,)), ((), ())), preferred_element_type=jnp.float32
            ).astype(out_ref.dtype)


def hidden_grad_parts(grad_slots, head_slots):
    return pl.pallas_call(
        hidden_grad_kernel,
        out_shape=jax.ShapeDtypeStruct((16, 128, 256), jnp.bfloat16),
        name="hidden_grad",
    )(*grad_slots, *head_slots)


def shards(teacher_hidden, teacher_gain, teacher_head, student_hidden, student_head, depth_cut):
    f32, f16, bf16 = jnp.float32, jnp.float16, jnp.bfloat16
    zl = lax.axis_index("group")
    dp, mp = lax.axis_index("dp"), lax.axis_index("mp")
    y, zh, x, core = dp // 4, dp % 4, mp // 2, mp % 2

    steps = jnp.arange(4, dtype=jnp.int32)
    order = (((y - steps) % 4 * 4)[None, :] + ((zh + steps) % 4)[:, None]).reshape(16)
    blocks = picked_blocks(student_hidden, order).reshape(4, 4, 128, 256)
    hidden_slots = [blocks[0]] + [to_zh(blocks[k], k) for k in (1, 2, 3)]
    head_slots = [student_head] + [to_y(student_head, j) for j in (1, 2, 3)]

    hidden_float = teacher_hidden.astype(f32)
    own_squares = jnp.sum(hidden_float * hidden_float, axis=1)
    squares = lax.all_to_all(
        jnp.broadcast_to(own_squares[None, None], (16, 1, 128)), PLANE, 0, 0, tiled=True
    ).sum(axis=(0, 1))
    row_scale = lax.rsqrt(squares / DT + epsilon)
    normed = (hidden_float * row_scale[:, None] * teacher_gain.astype(f32)[None, :]).astype(bf16)
    spots = jnp.arange(16, dtype=jnp.int32)
    order = (zl ^ (spots % 2)) * 8 + (x + spots // 2 % 4) % 4 * 2 + (core ^ (spots // 8))
    parts = teacher_parts(normed, teacher_head, order).reshape(2, 4, 2, 128, 512)
    by_core = parts[0] + to_core(parts[1].astype(f16)).astype(f32)
    by_x = by_core[0]
    for step in (1, 2, 3):
        by_x = by_x + to_x(by_core[step].astype(f16), step).astype(f32)
    teacher = by_x[0] + to_zl(by_x[1].astype(f16)).astype(f32)

    parts = student_parts(hidden_slots, head_slots)
    student = parts[0]
    for k in (1, 2, 3):
        student = student + to_zh(parts[k].astype(f16), -k).astype(f32)

    teacher_max = jnp.max(teacher, axis=1)
    student_max = jnp.max(student, axis=1)
    teacher_exp = jnp.exp(teacher - teacher_max[:, None])
    student_exp = jnp.exp(student - student_max[:, None])
    stats = jnp.stack(
        [
            teacher_max,
            jnp.sum(teacher_exp, axis=1),
            jnp.sum(teacher_exp * (teacher - student), axis=1),
            student_max,
            jnp.sum(student_exp, axis=1),
        ]
    )
    every = jnp.stack(
        [
            stats,
            to_core(stats),
            send(stats, lambda zl, y, zh, x, core: (zl, y, zh, x ^ 1, core)),
            send(stats, lambda zl, y, zh, x, core: (zl, y, zh, x ^ 1, 1 - core)),
        ]
    )
    teacher_top = jnp.max(every[:, 0], axis=0)
    student_top = jnp.max(every[:, 3], axis=0)
    teacher_shift = jnp.exp(every[:, 0] - teacher_top)
    student_shift = jnp.exp(every[:, 3] - student_top)
    teacher_sum = jnp.sum(every[:, 1] * teacher_shift, axis=0)
    student_sum = jnp.sum(every[:, 4] * student_shift, axis=0)
    weighted = jnp.sum(every[:, 2] * teacher_shift, axis=0)
    divergence = (
        weighted / teacher_sum - (teacher_top + jnp.log(teacher_sum)) + (student_top + jnp.log(student_sum))
    )
    book = zl * 2 + x // 2
    depth_rows = jnp.repeat(depth_cut, FRAMES)
    depth_weight = (book < depth_rows).astype(f32) / depth_rows.astype(f32)
    teacher_factor = teacher_shift[0] / teacher_sum * depth_weight
    student_factor = student_shift[0] / student_sum * depth_weight
    score_grad = (
        student_exp * student_factor[:, None] - teacher_exp * teacher_factor[:, None]
    ).astype(bf16)

    own_kl = (divergence * depth_weight)[None]
    kl = jnp.concatenate(
        [
            own_kl,
            send(own_kl, lambda zl, y, zh, x, core: (zl, y, zh, x ^ 2, core)),
            send(own_kl, lambda zl, y, zh, x, core: (1 - zl, y, zh, x, core)),
            send(own_kl, lambda zl, y, zh, x, core: (1 - zl, y, zh, x ^ 2, core)),
        ]
    )
    kl_terms = jnp.concatenate(
        [lax.dynamic_slice_in_dim(kl, book ^ i, 1, 0) for i in range(C)]
    )

    grad_slots = [score_grad] + [to_zh(score_grad, k) for k in (1, 2, 3)]
    head_grad, parts = head_grad_parts(hidden_slots, grad_slots)
    for j in (1, 2, 3):
        head_grad = head_grad + to_y(parts[j - 1], -j).astype(f32)
    parts = hidden_grad_parts(grad_slots, head_slots)
    parts = lax.all_to_all(parts, PLANE, 0, 0, tiled=True)
    hidden_grad = jnp.sum(parts.astype(f32), axis=0)

    def home(zl, y, zh, x, core):
        k, j = zl * 2 + x // 2, x % 2 * 2 + core
        spot = (y - j) % 4 * 4 + zh
        return spot // 8, y, zh - k, spot % 8 // 2, spot % 2

    hidden_grad = send(hidden_grad, home)
    return (kl_terms, hidden_grad, head_grad)


def solution(mesh):
    return jax.shard_map(
        shards,
        mesh=mesh,
        in_specs=(
            P("dp", PLANE),
            P(PLANE),
            P(PLANE, None),
            P("dp", None),
            P("dp", PLANE),
            P("dp"),
        ),
        out_specs=(P(None, "dp"), P("dp", PLANE), P("dp", PLANE)),
        check_vma=False,
    )
```

```python
import jax
import jax.numpy as jnp
from jax import lax
from jax.experimental import pallas as pl
from jax.experimental.pallas import tpu as pltpu
from jax.sharding import PartitionSpec as P

DT = 8192
C = 4
FRAMES = 64
epsilon = 1e-05

ALL = ("group", "dp", "mp")
PLANE = ("group", "mp")


def place(zl, y, zh, x, core):
    return zl * 128 + (y % 4 * 4 + zh % 4) * 8 + x % 4 * 2 + core


def send(value, target):
    pairs = []
    for zl in range(2):
        for y in range(4):
            for zh in range(4):
                for x in range(4):
                    for core in range(2):
                        pairs.append((place(zl, y, zh, x, core), place(*target(zl, y, zh, x, core))))
    return lax.ppermute(value, ALL, pairs)


def to_y(value, step):
    return send(value, lambda zl, y, zh, x, core: (zl, y + step, zh, x, core))


def to_zh(value, step):
    return send(value, lambda zl, y, zh, x, core: (zl, y, zh + step, x, core))


def to_x(value, step):
    return send(value, lambda zl, y, zh, x, core: (zl, y, zh, x + step, core))


def to_zl(value):
    return send(value, lambda zl, y, zh, x, core: (1 - zl, y, zh, x, core))


def to_core(value):
    return send(value, lambda zl, y, zh, x, core: (zl, y, zh, x, 1 - core))


def pick_kernel(order_ref, hidden_ref, own_ref, *half_refs):
    def block(i):
        return hidden_ref[:, pl.ds(pl.multiple_of(order_ref[i] * 256, 256), 256)]

    for p in range(4):
        own_ref[p] = block(p)
    for k in (1, 2, 3):
        for p in range(2):
            half_refs[k - 1][p] = block(4 * k + p)


def picked_blocks(hidden, order):
    rows = hidden.shape[0]
    half = jax.ShapeDtypeStruct((2, rows, 256), hidden.dtype)
    return pl.pallas_call(
        pick_kernel,
        in_specs=[pl.BlockSpec(memory_space=pltpu.SMEM), pl.BlockSpec(memory_space=pltpu.VMEM)],
        out_shape=(jax.ShapeDtypeStruct((4, rows, 256), hidden.dtype), half, half, half),
        name="pick",
    )(order, hidden)


def teacher_kernel(order_ref, normed_ref, head_ref, out_ref):
    core = order_ref[8]
    scores = jnp.dot(normed_ref[...], head_ref[...], preferred_element_type=jnp.float32)
    for k in range(2):
        out_ref[k ^ core, 0] = scores[:, 512 * k : 512 * (k + 1)]


def teacher_parts(normed, head, order):
    rows, depth = normed.shape
    return pl.pallas_call(
        teacher_kernel,
        grid_spec=pltpu.PrefetchScalarGridSpec(
            num_scalar_prefetch=1,
            grid=(8,),
            in_specs=[
                pl.BlockSpec((rows, depth), lambda i, order_ref: (0, 0)),
                pl.BlockSpec((depth, 1024), lambda i, order_ref: (0, order_ref[i])),
            ],
            out_specs=pl.BlockSpec((2, 1, rows, 512), lambda i, order_ref: (0, i, 0, 0)),
        ),
        out_shape=jax.ShapeDtypeStruct((2, 8, rows, 512), jnp.float32),
        name="teacher",
    )(order, normed, head)


def student_kernel(core_ref, *refs):
    own_ref, near_refs, far_refs, head_refs = refs[0], refs[1:4], refs[4:7], refs[7:11]
    out_ref, hidden_ref = refs[11:]
    core = core_ref[0]
    for p in range(2):
        hidden_ref[0, 2 * core + p] = own_ref[p]
        hidden_ref[0, 2 * (1 - core) + p] = own_ref[2 + p]
        for k in (1, 2, 3):
            hidden_ref[k, 2 * core + p] = near_refs[k - 1][p]
            hidden_ref[k, 2 * (1 - core) + p] = far_refs[k - 1][p]
    for k in range(4):
        total = None
        for j in range(4):
            term = jnp.dot(hidden_ref[k, j], head_refs[j][...], preferred_element_type=jnp.float32)
            total = term if total is None else total + term
        out_ref[k] = total


def student_parts(core, own, near, far, head_slots):
    vmem = pl.BlockSpec(memory_space=pltpu.VMEM)
    return pl.pallas_call(
        student_kernel,
        in_specs=[pl.BlockSpec(memory_space=pltpu.SMEM)] + [vmem] * 11,
        out_shape=(
            jax.ShapeDtypeStruct((4, 128, 512), jnp.float32),
            jax.ShapeDtypeStruct((4, 4, 128, 256), jnp.bfloat16),
        ),
        name="student",
    )(core.reshape(1), own, *near, *far, *head_slots)


def head_grad_kernel(*refs):
    hidden_ref, grad_refs, own_ref, out_ref = refs[0], refs[1:5], refs[5], refs[6]
    for j in range(4):
        total = None
        for k in range(4):
            term = lax.dot_general(
                hidden_ref[k, j], grad_refs[k][...], (((0,), (0,)), ((), ())), preferred_element_type=jnp.float32
            )
            total = term if total is None else total + term
        if j == 0:
            own_ref[...] = total
        else:
            out_ref[j - 1] = total.astype(out_ref.dtype)


def head_grad_parts(hidden, grad_slots):
    return pl.pallas_call(
        head_grad_kernel,
        out_shape=(
            jax.ShapeDtypeStruct((256, 512), jnp.float32),
            jax.ShapeDtypeStruct((3, 256, 512), jnp.bfloat16),
        ),
        name="head_grad",
    )(hidden, *grad_slots)


def hidden_grad_kernel(*refs):
    grad_refs, head_refs, out_ref = refs[:4], refs[4:8], refs[8]
    for k in range(4):
        for j in range(4):
            out_ref[4 * k + j] = lax.dot_general(
                grad_refs[k][...], head_refs[j][...], (((1,), (1,)), ((), ())), preferred_element_type=jnp.float32
            ).astype(out_ref.dtype)


def hidden_grad_parts(grad_slots, head_slots):
    return pl.pallas_call(
        hidden_grad_kernel,
        out_shape=jax.ShapeDtypeStruct((16, 128, 256), jnp.bfloat16),
        name="hidden_grad",
    )(*grad_slots, *head_slots)


def step(teacher_hidden, teacher_gain, teacher_head, student_hidden, student_head, depth_cut):
    f32, f16, bf16 = jnp.float32, jnp.float16, jnp.bfloat16
    zl = lax.axis_index("group")
    dp, mp = lax.axis_index("dp"), lax.axis_index("mp")
    y, zh, x, core = dp // 4, dp % 4, mp // 2, mp % 2

    hidden_float = teacher_hidden.astype(f32)
    own_squares = jnp.sum(hidden_float * hidden_float, axis=1)
    squares = lax.all_to_all(
        jnp.broadcast_to(own_squares[None, None], (16, 1, 128)), PLANE, 0, 0, tiled=True
    ).sum(axis=(0, 1))

    steps = jnp.arange(4, dtype=jnp.int32)
    order = (((y - steps - 2 * core) % 4 * 4)[None, :] + ((zh + steps) % 4)[:, None]).reshape(16)
    own, *halves = picked_blocks(student_hidden, order)
    near = [to_zh(halves[k - 1], k) for k in (1, 2, 3)]
    head_slots = [student_head] + [to_y(student_head, j) for j in (1, 2, 3)]
    far = [to_core(half) for half in near]

    row_scale = lax.rsqrt(squares / DT + epsilon)
    normed = (hidden_float * row_scale[:, None] * teacher_gain.astype(f32)[None, :]).astype(bf16)
    spots = jnp.arange(8, dtype=jnp.int32)
    order = (zl ^ (spots % 2)) * 4 + (x + spots // 2) % 4
    parts = teacher_parts(normed, teacher_head, jnp.append(order, core)).reshape(2, 4, 2, 128, 512)
    by_core = parts[0] + to_core(parts[1].astype(f16)).astype(f32)
    by_x = by_core[0]
    for step in (1, 2, 3):
        by_x = by_x + to_x(by_core[step].astype(f16), step).astype(f32)
    teacher = by_x[0] + to_zl(by_x[1].astype(f16)).astype(f32)

    parts, hidden = student_parts(core, own, near, far, head_slots)
    student = parts[0]
    for k in (1, 2, 3):
        student = student + to_zh(parts[k].astype(f16), -k).astype(f32)

    teacher_max = jnp.max(teacher, axis=1)
    student_max = jnp.max(student, axis=1)
    teacher_exp = jnp.exp(teacher - teacher_max[:, None])
    student_exp = jnp.exp(student - student_max[:, None])
    stats = jnp.stack(
        [
            teacher_max,
            jnp.sum(teacher_exp, axis=1),
            jnp.sum(teacher_exp * (teacher - student), axis=1),
            student_max,
            jnp.sum(student_exp, axis=1),
        ]
    )
    every = jnp.stack(
        [
            stats,
            to_core(stats),
            send(stats, lambda zl, y, zh, x, core: (zl, y, zh, x ^ 1, core)),
            send(stats, lambda zl, y, zh, x, core: (zl, y, zh, x ^ 1, 1 - core)),
        ]
    )
    teacher_top = jnp.max(every[:, 0], axis=0)
    student_top = jnp.max(every[:, 3], axis=0)
    teacher_shift = jnp.exp(every[:, 0] - teacher_top)
    student_shift = jnp.exp(every[:, 3] - student_top)
    teacher_sum = jnp.sum(every[:, 1] * teacher_shift, axis=0)
    student_sum = jnp.sum(every[:, 4] * student_shift, axis=0)
    weighted = jnp.sum(every[:, 2] * teacher_shift, axis=0)
    divergence = (
        weighted / teacher_sum - (teacher_top + jnp.log(teacher_sum)) + (student_top + jnp.log(student_sum))
    )
    book = zl * 2 + x // 2
    depth_rows = jnp.repeat(depth_cut, FRAMES)
    depth_weight = (book < depth_rows).astype(f32) / depth_rows.astype(f32)
    teacher_factor = teacher_shift[0] / teacher_sum * depth_weight
    student_factor = student_shift[0] / student_sum * depth_weight
    score_grad = (
        student_exp * student_factor[:, None] - teacher_exp * teacher_factor[:, None]
    ).astype(bf16)

    own_kl = (divergence * depth_weight)[None]
    kl = [
        own_kl,
        send(own_kl, lambda zl, y, zh, x, core: (zl, y, zh, x ^ 2, core)),
        send(own_kl, lambda zl, y, zh, x, core: (1 - zl, y, zh, x, core)),
        send(own_kl, lambda zl, y, zh, x, core: (1 - zl, y, zh, x ^ 2, core)),
    ]
    kl = jnp.concatenate(kl)
    kl_terms = jnp.concatenate(
        [lax.dynamic_slice_in_dim(kl, book ^ i, 1, 0) for i in range(C)]
    )

    grad_slots = [score_grad] + [to_zh(score_grad, k) for k in (1, 2, 3)]
    parts = hidden_grad_parts(grad_slots, head_slots)
    parts = lax.all_to_all(parts, PLANE, 0, 0, tiled=True)
    hidden_grad = jnp.sum(parts.astype(f32), axis=0)
    head_grad, parts = head_grad_parts(hidden, grad_slots)
    for j in (1, 2, 3):
        head_grad = head_grad + to_y(parts[j - 1], -j).astype(f32)

    def home(zl, y, zh, x, core):
        k, j = zl * 2 + x // 2, x % 2 * 2 + core
        spot = (y - j) % 4 * 4 + zh
        return spot // 8, y, zh - k, spot % 8 // 2, spot % 2

    hidden_grad = send(hidden_grad, home)
    return (kl_terms, hidden_grad, head_grad)


def solution(mesh):
    return jax.shard_map(
        step,
        mesh=mesh,
        in_specs=(
            P("dp", PLANE),
            P(PLANE),
            P(PLANE, None),
            P("dp", None),
            P("dp", PLANE),
            P("dp"),
        ),
        out_specs=(P(None, "dp"), P("dp", PLANE), P("dp", PLANE)),
        check_vma=False,
    )
```

```python
import jax
import jax.numpy as jnp
from jax import lax
from jax.experimental import pallas as pl
from jax.experimental.pallas import tpu as pltpu
from jax.sharding import PartitionSpec as P

DT = 8192
C = 4
FRAMES = 64
epsilon = 1e-05

ALL = ("group", "dp", "mp")
PLANE = ("group", "mp")


def place(zl, y, zh, x, core):
    return zl * 128 + (y % 4 * 4 + zh % 4) * 8 + x % 4 * 2 + core


def send(value, target):
    pairs = []
    for zl in range(2):
        for y in range(4):
            for zh in range(4):
                for x in range(4):
                    for core in range(2):
                        pairs.append((place(zl, y, zh, x, core), place(*target(zl, y, zh, x, core))))
    return lax.ppermute(value, ALL, pairs)


def to_y(value, step):
    return send(value, lambda zl, y, zh, x, core: (zl, y + step, zh, x, core))


def to_zh(value, step):
    return send(value, lambda zl, y, zh, x, core: (zl, y, zh + step, x, core))


def to_x(value, step):
    return send(value, lambda zl, y, zh, x, core: (zl, y, zh, x + step, core))


def to_zl(value):
    return send(value, lambda zl, y, zh, x, core: (1 - zl, y, zh, x, core))


def to_core(value):
    return send(value, lambda zl, y, zh, x, core: (zl, y, zh, x, 1 - core))


def pick_kernel(order_ref, hidden_ref, own_ref, *half_refs):
    def block(i):
        return hidden_ref[:, pl.ds(pl.multiple_of(order_ref[i] * 256, 256), 256)]

    for p in range(4):
        own_ref[p] = block(p)
    for k in (1, 2, 3):
        for p in range(2):
            half_refs[k - 1][p] = block(4 * k + p)


def picked_blocks(hidden, order):
    rows = hidden.shape[0]
    half = jax.ShapeDtypeStruct((2, rows, 256), hidden.dtype)
    return pl.pallas_call(
        pick_kernel,
        in_specs=[pl.BlockSpec(memory_space=pltpu.SMEM), pl.BlockSpec(memory_space=pltpu.VMEM)],
        out_shape=(jax.ShapeDtypeStruct((4, rows, 256), hidden.dtype), half, half, half),
        name="pick",
    )(order, hidden)


def teacher_kernel(order_ref, hidden_ref, gain_ref, *refs):
    head_refs, out_ref, both_ref = refs[:4], refs[4], refs[5]
    rows = hidden_ref.shape[0]

    @pl.when(pl.program_id(0) == 0)
    def _():
        product = hidden_ref[...].astype(jnp.float32) * gain_ref[...].astype(jnp.float32)
        high = product.astype(jnp.bfloat16)
        both_ref[:rows] = high
        both_ref[rows:] = (product - high.astype(jnp.float32)).astype(jnp.bfloat16)

    for i in range(4):
        scores = jnp.dot(both_ref[...], head_refs[i][...], preferred_element_type=jnp.float32)
        out_ref[i] = scores[:rows] + scores[rows:]


def teacher_parts(hidden, gain, head, order):
    rows, depth = hidden.shape

    def block(n):
        return pl.BlockSpec((depth, 512), lambda i, order_ref: (0, order_ref[4 * i + n]))

    return pl.pallas_call(
        teacher_kernel,
        grid_spec=pltpu.PrefetchScalarGridSpec(
            num_scalar_prefetch=1,
            grid=(2,),
            in_specs=[
                pl.BlockSpec((rows, depth), lambda i, order_ref: (0, 0)),
                pl.BlockSpec((1, depth), lambda i, order_ref: (0, 0)),
                *(block(n) for n in range(4)),
            ],
            out_specs=pl.BlockSpec((4, rows, 512), lambda i, order_ref: (i, 0, 0)),
            scratch_shapes=[pltpu.VMEM((2 * rows, depth), jnp.bfloat16)],
        ),
        out_shape=jax.ShapeDtypeStruct((8, rows, 512), jnp.float32),
        name="teacher",
    )(order, hidden, gain[None], head, head, head, head)


def student_kernel(core_ref, *refs):
    own_ref, near_refs, far_refs, head_refs = refs[0], refs[1:4], refs[4:7], refs[7:11]
    out_refs, hidden_ref = refs[11:15], refs[15]
    core = core_ref[0]
    for p in range(2):
        hidden_ref[0, 2 * core + p] = own_ref[p]
        hidden_ref[0, 2 * (1 - core) + p] = own_ref[2 + p]
        for k in (1, 2, 3):
            hidden_ref[k, 2 * core + p] = near_refs[k - 1][p]
            hidden_ref[k, 2 * (1 - core) + p] = far_refs[k - 1][p]
    for k in range(4):
        total = None
        for j in range(4):
            term = jnp.dot(hidden_ref[k, j], head_refs[j][...], preferred_element_type=jnp.float32)
            total = term if total is None else total + term
        out_refs[k][...] = total


def student_parts(core, own, near, far, head_slots):
    vmem = pl.BlockSpec(memory_space=pltpu.VMEM)
    return pl.pallas_call(
        student_kernel,
        in_specs=[pl.BlockSpec(memory_space=pltpu.SMEM)] + [vmem] * 11,
        out_shape=(
            *[jax.ShapeDtypeStruct((128, 512), jnp.float32)] * 4,
            jax.ShapeDtypeStruct((4, 4, 128, 256), jnp.bfloat16),
        ),
        name="student",
    )(core.reshape(1), own, *near, *far, *head_slots)


def head_grad_kernel(*refs):
    hidden_ref, grad_refs, own_ref, out_refs = refs[0], refs[1:5], refs[5], refs[6:]
    for j in range(4):
        total = None
        for k in range(4):
            term = lax.dot_general(
                hidden_ref[k, j], grad_refs[k][...], (((0,), (0,)), ((), ())), preferred_element_type=jnp.float32
            )
            total = term if total is None else total + term
        if j == 0:
            own_ref[...] = total
        else:
            out_refs[j - 1][...] = total.astype(jnp.bfloat16)


def head_grad_parts(hidden, grad_slots):
    return pl.pallas_call(
        head_grad_kernel,
        out_shape=(
            jax.ShapeDtypeStruct((256, 512), jnp.float32),
            *[jax.ShapeDtypeStruct((256, 512), jnp.bfloat16)] * 3,
        ),
        name="head_grad",
    )(hidden, *grad_slots)


def hidden_grad_kernel(*refs):
    grad_refs, head_refs, out_ref = refs[:3], refs[3:7], refs[7]
    for k in range(3):
        for j in range(4):
            out_ref[4 * k + j] = lax.dot_general(
                grad_refs[k][...], head_refs[j][...], (((1,), (1,)), ((), ())), preferred_element_type=jnp.float32
            ).astype(out_ref.dtype)


def last_hidden_grad_kernel(parts_ref, grad_ref, *refs):
    head_refs, out_ref = refs[:4], refs[4]
    for j in range(4):
        out_ref[j] = lax.dot_general(
            grad_ref[...], head_refs[j][...], (((1,), (1,)), ((), ())), preferred_element_type=jnp.float32
        ).astype(out_ref.dtype)


def hidden_grad_parts(grad_slots, head_slots):
    shape = jax.ShapeDtypeStruct((16, 128, 256), jnp.bfloat16)
    parts = pl.pallas_call(hidden_grad_kernel, out_shape=shape, name="hidden_grad")(*grad_slots[:3], *head_slots)
    return pl.pallas_call(
        last_hidden_grad_kernel,
        grid=(1,),
        in_specs=[
            pl.BlockSpec(memory_space=pl.ANY),
            pl.BlockSpec((128, 512), lambda i: (0, 0)),
            *[pl.BlockSpec((256, 512), lambda i: (0, 0))] * 4,
        ],
        out_specs=pl.BlockSpec((4, 128, 256), lambda i: (3, 0, 0)),
        out_shape=shape,
        input_output_aliases={0: 0},
        name="last_hidden_grad",
    )(parts, grad_slots[3], *head_slots)


def step(teacher_hidden, teacher_gain, teacher_head, student_hidden, student_head, depth_cut):
    f32, f16, bf16 = jnp.float32, jnp.float16, jnp.bfloat16
    zl = lax.axis_index("group")
    dp, mp = lax.axis_index("dp"), lax.axis_index("mp")
    y, zh, x, core = dp // 4, dp % 4, mp // 2, mp % 2

    steps = jnp.arange(4, dtype=jnp.int32)
    order = (((y - steps - 2 * core) % 4 * 4)[None, :] + ((zh + steps) % 4)[:, None]).reshape(16)
    own, *halves = picked_blocks(student_hidden, order)
    near = [to_zh(halves[k - 1], k) for k in (1, 2, 3)]
    head_slots = [student_head] + [to_y(student_head, j) for j in (1, 2, 3)]
    far = [to_core(half) for half in near]

    spots = jnp.arange(8, dtype=jnp.int32)
    order = ((zl ^ (spots % 2)) * 4 + (x + spots // 2) % 4) * 2
    other = teacher_parts(teacher_hidden, teacher_gain, teacher_head, order + (1 - core))
    other = to_core(other)
    parts = teacher_parts(teacher_hidden, teacher_gain, teacher_head, order + core)
    by_x = parts[:2] + other[:2]
    for step in (1, 2, 3):
        part = parts[2 * step : 2 * step + 2] + other[2 * step : 2 * step + 2]
        by_x = by_x + to_x(part.astype(f16), step).astype(f32)
    teacher = by_x[0] + to_zl(by_x[1].astype(f16)).astype(f32)

    *parts, hidden = student_parts(core, own, near, far, head_slots)
    student = parts[0]
    for k in (1, 2, 3):
        student = student + to_zh(parts[k].astype(f16), -k).astype(f32)

    hidden_float = teacher_hidden.astype(f32)
    own_squares = jnp.sum(hidden_float * hidden_float, axis=1)
    squares = lax.all_to_all(
        jnp.broadcast_to(own_squares[None, None], (16, 1, 128)), PLANE, 0, 0, tiled=True
    ).sum(axis=(0, 1))
    row_scale = lax.rsqrt(squares / DT + epsilon)
    teacher = teacher * row_scale[:, None]

    teacher_max = jnp.max(teacher, axis=1)
    student_max = jnp.max(student, axis=1)
    teacher_exp = jnp.exp(teacher - teacher_max[:, None])
    student_exp = jnp.exp(student - student_max[:, None])
    stats = jnp.stack(
        [
            teacher_max,
            jnp.sum(teacher_exp, axis=1),
            jnp.sum(teacher_exp * (teacher - student), axis=1),
            student_max,
            jnp.sum(student_exp, axis=1),
        ]
    )
    every = jnp.stack(
        [
            stats,
            to_core(stats),
            send(stats, lambda zl, y, zh, x, core: (zl, y, zh, x ^ 1, core)),
            send(stats, lambda zl, y, zh, x, core: (zl, y, zh, x ^ 1, 1 - core)),
        ]
    )
    teacher_top = jnp.max(every[:, 0], axis=0)
    student_top = jnp.max(every[:, 3], axis=0)
    teacher_shift = jnp.exp(every[:, 0] - teacher_top)
    student_shift = jnp.exp(every[:, 3] - student_top)
    teacher_sum = jnp.sum(every[:, 1] * teacher_shift, axis=0)
    student_sum = jnp.sum(every[:, 4] * student_shift, axis=0)
    weighted = jnp.sum(every[:, 2] * teacher_shift, axis=0)
    divergence = (
        weighted / teacher_sum - (teacher_top + jnp.log(teacher_sum)) + (student_top + jnp.log(student_sum))
    )
    book = zl * 2 + x // 2
    depth_rows = jnp.repeat(depth_cut, FRAMES)
    depth_weight = (book < depth_rows).astype(f32) / depth_rows.astype(f32)
    teacher_factor = teacher_shift[0] / teacher_sum * depth_weight
    student_factor = student_shift[0] / student_sum * depth_weight
    score_grad = (
        student_exp * student_factor[:, None] - teacher_exp * teacher_factor[:, None]
    ).astype(bf16)

    own_kl = (divergence * depth_weight)[None]
    kl = [
        own_kl,
        send(own_kl, lambda zl, y, zh, x, core: (zl, y, zh, x ^ 2, core)),
        send(own_kl, lambda zl, y, zh, x, core: (1 - zl, y, zh, x, core)),
        send(own_kl, lambda zl, y, zh, x, core: (1 - zl, y, zh, x ^ 2, core)),
    ]
    kl = jnp.concatenate(kl)
    kl_terms = jnp.concatenate(
        [lax.dynamic_slice_in_dim(kl, book ^ i, 1, 0) for i in range(C)]
    )

    grad_slots = [score_grad] + [to_zh(score_grad, k) for k in (1, 2, 3)]
    parts = hidden_grad_parts(grad_slots, head_slots)
    parts = lax.all_to_all(parts, PLANE, 0, 0, tiled=True)
    hidden_grad = jnp.sum(parts.astype(f32), axis=0)
    head_grad, *parts = head_grad_parts(hidden, grad_slots)
    for j in (1, 2, 3):
        head_grad = head_grad + to_y(parts[j - 1], -j).astype(f32)

    def home(zl, y, zh, x, core):
        k, j = zl * 2 + x // 2, x % 2 * 2 + core
        spot = (y - j) % 4 * 4 + zh
        return spot // 8, y, zh - k, spot % 8 // 2, spot % 2

    hidden_grad = send(hidden_grad, home)
    return (kl_terms, hidden_grad, head_grad)


def solution(mesh):
    return jax.shard_map(
        step,
        mesh=mesh,
        in_specs=(
            P("dp", PLANE),
            P(PLANE),
            P(PLANE, None),
            P("dp", None),
            P("dp", PLANE),
            P("dp"),
        ),
        out_specs=(P(None, "dp"), P("dp", PLANE), P("dp", PLANE)),
        check_vma=False,
    )
```

```python
import jax
import jax.numpy as jnp
from jax import lax
from jax.experimental import pallas as pl
from jax.experimental.pallas import tpu as pltpu
from jax.sharding import PartitionSpec as P

DT = 8192
C = 4
FRAMES = 64
epsilon = 1e-05

ALL = ("group", "dp", "mp")
PLANE = ("group", "mp")


def place(zl, y, zh, x, core):
    return zl * 128 + (y % 4 * 4 + zh % 4) * 8 + x % 4 * 2 + core


def send(value, target):
    pairs = []
    for zl in range(2):
        for y in range(4):
            for zh in range(4):
                for x in range(4):
                    for core in range(2):
                        pairs.append((place(zl, y, zh, x, core), place(*target(zl, y, zh, x, core))))
    return lax.ppermute(value, ALL, pairs)


def to_y(value, step):
    return send(value, lambda zl, y, zh, x, core: (zl, y + step, zh, x, core))


def to_zh(value, step):
    return send(value, lambda zl, y, zh, x, core: (zl, y, zh + step, x, core))


def to_x(value, step):
    return send(value, lambda zl, y, zh, x, core: (zl, y, zh, x + step, core))


def to_zl(value):
    return send(value, lambda zl, y, zh, x, core: (1 - zl, y, zh, x, core))


def to_core(value):
    return send(value, lambda zl, y, zh, x, core: (zl, y, zh, x, 1 - core))


def coordinates(index):
    return index // 128, index // 32 % 4, index // 8 % 4, index // 2 % 4, index % 2


def pick_kernel(index_ref, hidden_ref, own_ref, *half_refs):
    _, y, zh, _, core = coordinates(index_ref[0])

    def block(k, p):
        spot = (y + 8 - p - 2 * core) % 4 * 4 + (zh + k) % 4
        return hidden_ref[:, pl.ds(pl.multiple_of(spot * 256, 256), 256)]

    for p in range(4):
        own_ref[p] = block(0, p)
    for k in (1, 2, 3):
        for p in range(2):
            half_refs[k - 1][p] = block(k, p)


def picked_blocks(index, hidden):
    rows = hidden.shape[0]
    half = jax.ShapeDtypeStruct((2, rows, 256), hidden.dtype)
    return pl.pallas_call(
        pick_kernel,
        in_specs=[pl.BlockSpec(memory_space=pltpu.SMEM), pl.BlockSpec(memory_space=pltpu.VMEM)],
        out_shape=(jax.ShapeDtypeStruct((4, rows, 256), hidden.dtype), half, half, half),
        name="pick",
    )(index, hidden)


def split(value):
    high = value.astype(jnp.bfloat16)
    return high, (value - high.astype(jnp.float32)).astype(jnp.bfloat16)


def teacher_kernel(index_ref, hidden_ref, gain_ref, *refs):
    head_refs, out_ref, both_ref, squares_ref = refs[:4], refs[4], refs[5], refs[6]
    rows, depth = hidden_ref.shape

    @pl.when(pl.program_id(0) == 0)
    def _():
        hidden = hidden_ref[...].astype(jnp.float32)
        high, low = split(hidden * gain_ref[...].astype(jnp.float32).reshape(1, depth))
        both_ref[:rows] = high
        both_ref[rows:] = low
        eighth = jnp.full((8, depth), 0.125, jnp.bfloat16)
        squares = sum(
            lax.dot_general(eighth, part, (((1,), (1,)), ((), ())), preferred_element_type=jnp.float32)
            for part in split(hidden * hidden)
        )
        squares_ref[...] = jnp.zeros_like(squares_ref)
        squares_ref[:, :rows] = squares

    for i in range(4):
        scores = jnp.dot(both_ref[...], head_refs[i][...], preferred_element_type=jnp.float32)
        out_ref[i, :rows] = scores[:rows] + scores[rows:]
        out_ref[i, rows:] = squares_ref[...]


def teacher_parts(index, hidden, gain, head, other):
    rows, depth = hidden.shape

    def block(n):
        def spot(i, index_ref):
            zl, _, _, x, core = coordinates(index_ref[0])
            zl = (zl + n) % 2
            return 0, (zl * 4 + (x + 2 * i + n // 2) % 4) * 2 + (core + other) % 2

        return pl.BlockSpec((depth, 512), spot)

    return pl.pallas_call(
        teacher_kernel,
        grid_spec=pltpu.PrefetchScalarGridSpec(
            num_scalar_prefetch=1,
            grid=(2,),
            in_specs=[
                pl.BlockSpec((rows, depth), lambda i, index_ref: (0, 0)),
                pl.BlockSpec((depth,), lambda i, index_ref: (0,)),
                *(block(n) for n in range(4)),
            ],
            out_specs=pl.BlockSpec((4, rows + 8, 512), lambda i, index_ref: (i, 0, 0)),
            scratch_shapes=[pltpu.VMEM((2 * rows, depth), jnp.bfloat16), pltpu.VMEM((8, 512), jnp.float32)],
        ),
        out_shape=jax.ShapeDtypeStruct((8, rows + 8, 512), jnp.float32),
        name="teacher",
    )(index, hidden, gain, head, head, head, head)


def student_kernel(index_ref, *refs):
    own_ref, near_refs, far_refs, head_refs = refs[0], refs[1:4], refs[4:7], refs[7:11]
    first_ref, out_ref, hidden_ref = refs[11:]
    core = index_ref[0] % 2
    for p in range(2):
        hidden_ref[0, 2 * core + p] = own_ref[p]
        hidden_ref[0, 2 * (1 - core) + p] = own_ref[2 + p]
        for k in (1, 2, 3):
            hidden_ref[k, 2 * core + p] = near_refs[k - 1][p]
            hidden_ref[k, 2 * (1 - core) + p] = far_refs[k - 1][p]
    for k in range(4):
        total = None
        for j in range(4):
            term = jnp.dot(hidden_ref[k, j], head_refs[j][...], preferred_element_type=jnp.float32)
            total = term if total is None else total + term
        if k == 0:
            first_ref[...] = total
        else:
            out_ref[k - 1] = total


def student_parts(index, own, near, far, head_slots):
    vmem = pl.BlockSpec(memory_space=pltpu.VMEM)
    return pl.pallas_call(
        student_kernel,
        in_specs=[pl.BlockSpec(memory_space=pltpu.SMEM)] + [vmem] * 11,
        out_shape=(
            jax.ShapeDtypeStruct((128, 512), jnp.float32),
            jax.ShapeDtypeStruct((3, 128, 512), jnp.float32),
            jax.ShapeDtypeStruct((4, 4, 128, 256), jnp.bfloat16),
        ),
        name="student",
    )(index, own, *near, *far, *head_slots)


def head_grad_kernel(*refs):
    hidden_ref, grad_refs, own_ref, out_refs = refs[0], refs[1:5], refs[5], refs[6:]
    for j in range(4):
        total = None
        for k in range(4):
            term = lax.dot_general(
                hidden_ref[k, j], grad_refs[k][...], (((0,), (0,)), ((), ())), preferred_element_type=jnp.float32
            )
            total = term if total is None else total + term
        if j == 0:
            own_ref[...] = total
        else:
            out_refs[j - 1][...] = total.astype(jnp.bfloat16)


def head_grad_parts(hidden, grad_slots):
    return pl.pallas_call(
        head_grad_kernel,
        out_shape=(
            jax.ShapeDtypeStruct((256, 512), jnp.float32),
            *[jax.ShapeDtypeStruct((256, 512), jnp.bfloat16)] * 3,
        ),
        name="head_grad",
    )(hidden, *grad_slots)


def hidden_grad_kernel(index_ref, *refs):
    grad_refs, head_refs, own_ref, other_ref = refs[:4], refs[4:8], refs[8], refs[9]
    zl, _, _, x, core = coordinates(index_ref[0])
    for k in range(4):
        for j in range(4):
            spot = (k % 2 * 2 + j // 2 + 4 - x) % 4 * 2 + (k // 2 + zl) % 2
            term = lax.dot_general(
                grad_refs[k][...], head_refs[j][...], (((1,), (1,)), ((), ())), preferred_element_type=jnp.float32
            )

            @pl.when(core == j % 2)
            def _():
                own_ref[spot] = term

            @pl.when(core != j % 2)
            def _():
                other_ref[spot] = term


def hidden_grad_parts(index, grad_slots, head_slots):
    vmem = pl.BlockSpec(memory_space=pltpu.VMEM)
    return pl.pallas_call(
        hidden_grad_kernel,
        in_specs=[pl.BlockSpec(memory_space=pltpu.SMEM)] + [vmem] * 8,
        out_shape=(jax.ShapeDtypeStruct((8, 128, 256), jnp.float32),) * 2,
        name="hidden_grad",
    )(index, *grad_slots, *head_slots)


def step(teacher_hidden, teacher_gain, teacher_head, student_hidden, student_head, depth_cut):
    f32, f16, bf16 = jnp.float32, jnp.float16, jnp.bfloat16
    zl = lax.axis_index("group")
    x = lax.axis_index("mp") // 2
    index = lax.axis_index(ALL).reshape(1)

    own, *halves = picked_blocks(index, student_hidden)
    near = [to_zh(halves[k - 1], k) for k in (1, 2, 3)]
    head_slots = [student_head] + [to_y(student_head, j) for j in (1, 2, 3)]
    far = [to_core(half) for half in near]

    other = teacher_parts(index, teacher_hidden, teacher_gain, teacher_head, 1)
    other = to_core(other)
    parts = teacher_parts(index, teacher_hidden, teacher_gain, teacher_head, 0)
    by_x = parts[:2] + other[:2]
    for step in (1, 2, 3):
        part = parts[2 * step : 2 * step + 2] + other[2 * step : 2 * step + 2]
        by_x = by_x + to_x(part.astype(f16), step).astype(f32)
    teacher = by_x[0] + to_zl(by_x[1].astype(f16)).astype(f32)

    student, parts, hidden = student_parts(index, own, near, far, head_slots)
    parts = parts.astype(f16)
    for k in (1, 2, 3):
        student = student + to_zh(parts[k - 1], -k).astype(f32)

    row_scale = lax.rsqrt(teacher[128, :128] * (8 / DT) + epsilon)
    teacher = teacher[:128] * row_scale[:, None]

    teacher_max = jnp.max(teacher, axis=1)
    student_max = jnp.max(student, axis=1)
    teacher_exp = jnp.exp(teacher - teacher_max[:, None])
    student_exp = jnp.exp(student - student_max[:, None])
    stats = jnp.stack(
        [
            teacher_max,
            jnp.sum(teacher_exp, axis=1),
            jnp.sum(teacher_exp * (teacher - student), axis=1),
            student_max,
            jnp.sum(student_exp, axis=1),
        ]
    )
    every = jnp.stack(
        [
            stats,
            to_core(stats),
            send(stats, lambda zl, y, zh, x, core: (zl, y, zh, x ^ 1, core)),
            send(stats, lambda zl, y, zh, x, core: (zl, y, zh, x ^ 1, 1 - core)),
        ]
    )
    teacher_top = jnp.max(every[:, 0], axis=0)
    student_top = jnp.max(every[:, 3], axis=0)
    teacher_shift = jnp.exp(every[:, 0] - teacher_top)
    student_shift = jnp.exp(every[:, 3] - student_top)
    teacher_sum = jnp.sum(every[:, 1] * teacher_shift, axis=0)
    student_sum = jnp.sum(every[:, 4] * student_shift, axis=0)
    weighted = jnp.sum(every[:, 2] * teacher_shift, axis=0)
    divergence = (
        weighted / teacher_sum - (teacher_top + jnp.log(teacher_sum)) + (student_top + jnp.log(student_sum))
    )
    book = zl * 2 + x // 2
    depth_rows = jnp.repeat(depth_cut, FRAMES)
    depth_weight = (book < depth_rows).astype(f32) / depth_rows.astype(f32)
    teacher_factor = teacher_shift[0] / teacher_sum * depth_weight
    student_factor = student_shift[0] / student_sum * depth_weight
    score_grad = (
        student_exp * student_factor[:, None] - teacher_exp * teacher_factor[:, None]
    ).astype(bf16)

    own_kl = (divergence * depth_weight)[None]
    kl = [
        own_kl,
        send(own_kl, lambda zl, y, zh, x, core: (zl, y, zh, x ^ 2, core)),
        send(own_kl, lambda zl, y, zh, x, core: (1 - zl, y, zh, x, core)),
        send(own_kl, lambda zl, y, zh, x, core: (1 - zl, y, zh, x ^ 2, core)),
    ]
    kl = jnp.concatenate(kl)
    kl_terms = jnp.concatenate(
        [lax.dynamic_slice_in_dim(kl, book ^ i, 1, 0) for i in range(C)]
    )

    grad_slots = [score_grad] + [to_zh(score_grad, k) for k in (1, 2, 3)]
    own, other = hidden_grad_parts(index, grad_slots, head_slots)
    other = to_core(other)
    head_grad, *parts = head_grad_parts(hidden, grad_slots)
    for j in (1, 2, 3):
        head_grad = head_grad + to_y(parts[j - 1], -j).astype(f32)
    by_x = own[:2] + other[:2]
    for step in (1, 2, 3):
        part = own[2 * step : 2 * step + 2] + other[2 * step : 2 * step + 2]
        by_x = by_x + to_x(part.astype(bf16), step).astype(f32)

    def home(zl, y, zh, x, core):
        k, j = zl * 2 + x // 2, x % 2 * 2 + core
        spot = (y - j) % 4 * 4 + zh
        return spot // 8, y, zh - k, spot % 8 // 2, spot % 2

    hidden_grad = send(by_x[0], home) + send(
        by_x[1], lambda zl, y, zh, x, core: home(1 - zl, y, zh, x, core)
    )
    return (kl_terms, hidden_grad, head_grad)


def solution(mesh):
    return jax.shard_map(
        step,
        mesh=mesh,
        in_specs=(
            P("dp", PLANE),
            P(PLANE),
            P(PLANE, None),
            P("dp", None),
            P("dp", PLANE),
            P("dp"),
        ),
        out_specs=(P(None, "dp"), P("dp", PLANE), P("dp", PLANE)),
        check_vma=False,
    )
```

```python
import jax
import jax.numpy as jnp
from jax import lax
from jax.experimental import pallas as pl
from jax.experimental.pallas import tpu as pltpu
from jax.sharding import PartitionSpec as P

DT = 8192
C = 4
FRAMES = 64
epsilon = 1e-05

ALL = ("group", "dp", "mp")
PLANE = ("group", "mp")


def place(zl, y, zh, x, core):
    return zl * 128 + (y % 4 * 4 + zh % 4) * 8 + x % 4 * 2 + core


def send(value, target):
    pairs = []
    for zl in range(2):
        for y in range(4):
            for zh in range(4):
                for x in range(4):
                    for core in range(2):
                        pairs.append((place(zl, y, zh, x, core), place(*target(zl, y, zh, x, core))))
    return lax.ppermute(value, ALL, pairs)


def to_y(value, step):
    return send(value, lambda zl, y, zh, x, core: (zl, y + step, zh, x, core))


def to_zh(value, step):
    return send(value, lambda zl, y, zh, x, core: (zl, y, zh + step, x, core))


def to_x(value, step):
    return send(value, lambda zl, y, zh, x, core: (zl, y, zh, x + step, core))


def to_zl(value):
    return send(value, lambda zl, y, zh, x, core: (1 - zl, y, zh, x, core))


def to_core(value):
    return send(value, lambda zl, y, zh, x, core: (zl, y, zh, x, 1 - core))


def coordinates(index):
    return index // 128, index // 32 % 4, index // 8 % 4, index // 2 % 4, index % 2


def hidden_block(k, p):
    def spot(i, index_ref):
        _, y, zh, _, core = coordinates(index_ref[0])
        return 0, (y + 8 - p - 2 * core) % 4 * 4 + (zh + k) % 4

    return pl.BlockSpec((128, 256), spot)


def pick_kernel(index_ref, *refs):
    block_refs, out_refs = refs[:6], refs[6:]
    for k in range(3):
        for p in range(2):
            out_refs[k][p] = block_refs[2 * k + p][...]


def picked_blocks(index, hidden):
    return pl.pallas_call(
        pick_kernel,
        grid_spec=pltpu.PrefetchScalarGridSpec(
            num_scalar_prefetch=1,
            grid=(1,),
            in_specs=[hidden_block(k, p) for k in (1, 2, 3) for p in range(2)],
            out_specs=[pl.BlockSpec((2, 128, 256), lambda i, index_ref: (0, 0, 0))] * 3,
        ),
        out_shape=[jax.ShapeDtypeStruct((2, 128, 256), hidden.dtype)] * 3,
        name="pick",
    )(index, *[hidden] * 6)


def split(value):
    high = value.astype(jnp.bfloat16)
    return high, (value - high.astype(jnp.float32)).astype(jnp.bfloat16)


def teacher_kernel(index_ref, hidden_ref, gain_ref, *refs):
    head_refs, out_ref, both_ref, squares_ref = refs[:4], refs[4], refs[5], refs[6]
    rows, depth = hidden_ref.shape

    @pl.when(pl.program_id(0) == 0)
    def _():
        hidden = hidden_ref[...].astype(jnp.float32)
        high, low = split(hidden * gain_ref[...].astype(jnp.float32).reshape(1, depth))
        both_ref[:rows] = high
        both_ref[rows:] = low
        eighth = jnp.full((8, depth), 0.125, jnp.bfloat16)
        squares = sum(
            lax.dot_general(eighth, part, (((1,), (1,)), ((), ())), preferred_element_type=jnp.float32)
            for part in split(hidden * hidden)
        )
        squares_ref[...] = jnp.zeros_like(squares_ref)
        squares_ref[:, :rows] = squares

    for i in range(4):
        scores = jnp.dot(both_ref[...], head_refs[i][...], preferred_element_type=jnp.float32)
        out_ref[i, :rows] = scores[:rows] + scores[rows:]
        out_ref[i, rows:] = squares_ref[...]


def teacher_parts(index, hidden, gain, head, other):
    rows, depth = hidden.shape

    def block(n):
        def spot(i, index_ref):
            zl, _, _, x, core = coordinates(index_ref[0])
            zl = (zl + n) % 2
            return 0, (zl * 4 + (x + 2 * i + n // 2) % 4) * 2 + (core + other) % 2

        return pl.BlockSpec((depth, 512), spot)

    return pl.pallas_call(
        teacher_kernel,
        grid_spec=pltpu.PrefetchScalarGridSpec(
            num_scalar_prefetch=1,
            grid=(2,),
            in_specs=[
                pl.BlockSpec((rows, depth), lambda i, index_ref: (0, 0)),
                pl.BlockSpec((depth,), lambda i, index_ref: (0,)),
                *(block(n) for n in range(4)),
            ],
            out_specs=pl.BlockSpec((4, rows + 8, 512), lambda i, index_ref: (i, 0, 0)),
            scratch_shapes=[pltpu.VMEM((2 * rows, depth), jnp.bfloat16), pltpu.VMEM((8, 512), jnp.float32)],
        ),
        out_shape=jax.ShapeDtypeStruct((8, rows + 8, 512), jnp.float32),
        name="teacher",
    )(index, hidden, gain, head, head, head, head)


def student_kernel(index_ref, *refs):
    own_refs, near_refs, far_refs, head_refs = refs[:4], refs[4:7], refs[7:10], refs[10:14]
    first_ref, out_ref, hidden_ref = refs[14:]
    core = index_ref[0] % 2
    for p in range(2):
        hidden_ref[0, 2 * core + p] = own_refs[p][...]
        hidden_ref[0, 2 * (1 - core) + p] = own_refs[2 + p][...]
        for k in (1, 2, 3):
            hidden_ref[k, 2 * core + p] = near_refs[k - 1][p]
            hidden_ref[k, 2 * (1 - core) + p] = far_refs[k - 1][p]
    for k in range(4):
        total = None
        for j in range(4):
            term = jnp.dot(hidden_ref[k, j], head_refs[j][...], preferred_element_type=jnp.float32)
            total = term if total is None else total + term
        if k == 0:
            first_ref[...] = total
        else:
            out_ref[k - 1] = total


def student_parts(index, own, near, far, head_slots):
    def whole(*shape):
        return pl.BlockSpec(shape, lambda i, index_ref: (0,) * len(shape))

    return pl.pallas_call(
        student_kernel,
        grid_spec=pltpu.PrefetchScalarGridSpec(
            num_scalar_prefetch=1,
            grid=(1,),
            in_specs=[hidden_block(0, p) for p in range(4)]
            + [whole(2, 128, 256)] * 6
            + [whole(256, 512)] * 4,
            out_specs=(whole(128, 512), whole(3, 128, 512), whole(4, 4, 128, 256)),
        ),
        out_shape=(
            jax.ShapeDtypeStruct((128, 512), jnp.float32),
            jax.ShapeDtypeStruct((3, 128, 512), jnp.float32),
            jax.ShapeDtypeStruct((4, 4, 128, 256), jnp.bfloat16),
        ),
        name="student",
    )(index, *[own] * 4, *near, *far, *head_slots)


def head_grad_kernel(*refs):
    hidden_ref, grad_refs, own_ref, out_refs = refs[0], refs[1:5], refs[5], refs[6:]
    for j in range(4):
        total = None
        for k in range(4):
            term = lax.dot_general(
                hidden_ref[k, j], grad_refs[k][...], (((0,), (0,)), ((), ())), preferred_element_type=jnp.float32
            )
            total = term if total is None else total + term
        if j == 0:
            own_ref[...] = total
        else:
            out_refs[j - 1][...] = total.astype(jnp.bfloat16)


def head_grad_parts(hidden, grad_slots):
    return pl.pallas_call(
        head_grad_kernel,
        out_shape=(
            jax.ShapeDtypeStruct((256, 512), jnp.float32),
            *[jax.ShapeDtypeStruct((256, 512), jnp.bfloat16)] * 3,
        ),
        name="head_grad",
    )(hidden, *grad_slots)


def hidden_grad_kernel(index_ref, *refs):
    grad_refs, head_refs, own_ref, other_ref, slots_ref = refs[:4], refs[4:8], refs[8], refs[9], refs[10]
    zl, y, zh, x, core = coordinates(index_ref[0])
    for k in range(4):
        slots_ref[k] = grad_refs[k][...]
    for m in range(2):
        for j in range(4):
            a = (y + 4 - j) % 4
            for out_ref, side in ((own_ref, core), (other_ref, 1 - core)):
                goal = 2 * m + side
                spot = (a % 2 * 2 + m + 4 - x) % 4 * 2 + (a // 2 + zl) % 2
                out_ref[spot] = lax.dot_general(
                    slots_ref[(zh + 4 - goal) % 4],
                    head_refs[j][...],
                    (((1,), (1,)), ((), ())),
                    preferred_element_type=jnp.float32,
                )


def hidden_grad_parts(index, grad_slots, head_slots):
    vmem = pl.BlockSpec(memory_space=pltpu.VMEM)
    return pl.pallas_call(
        hidden_grad_kernel,
        in_specs=[pl.BlockSpec(memory_space=pltpu.SMEM)] + [vmem] * 8,
        out_shape=(jax.ShapeDtypeStruct((8, 128, 256), jnp.float32),) * 2,
        scratch_shapes=[pltpu.VMEM((4, 128, 512), jnp.bfloat16)],
        name="hidden_grad",
    )(index, *grad_slots, *head_slots)


def step(teacher_hidden, teacher_gain, teacher_head, student_hidden, student_head, depth_cut):
    f32, f16, bf16 = jnp.float32, jnp.float16, jnp.bfloat16
    zl = lax.axis_index("group")
    x = lax.axis_index("mp") // 2
    index = lax.axis_index(ALL).reshape(1)

    halves = picked_blocks(index, student_hidden)
    near = [to_zh(halves[k - 1], k) for k in (1, 2, 3)]
    head_slots = [student_head] + [to_y(student_head, j) for j in (1, 2, 3)]
    far = [to_core(half) for half in near]

    other = teacher_parts(index, teacher_hidden, teacher_gain, teacher_head, 1)
    other = to_core(other)
    parts = teacher_parts(index, teacher_hidden, teacher_gain, teacher_head, 0)
    by_x = parts[:2] + other[:2]
    for step in (1, 2, 3):
        part = parts[2 * step : 2 * step + 2] + other[2 * step : 2 * step + 2]
        by_x = by_x + to_x(part.astype(f16), step).astype(f32)
    teacher = by_x[0] + to_zl(by_x[1].astype(f16)).astype(f32)

    student, parts, hidden = student_parts(index, student_hidden, near, far, head_slots)
    parts = parts.astype(f16)
    for k in (1, 2, 3):
        student = student + to_zh(parts[k - 1], -k).astype(f32)

    row_scale = lax.rsqrt(teacher[128, :128] * (8 / DT) + epsilon)
    teacher = teacher[:128] * row_scale[:, None]

    teacher_max = jnp.max(teacher, axis=1)
    student_max = jnp.max(student, axis=1)
    teacher_exp = jnp.exp(teacher - teacher_max[:, None])
    student_exp = jnp.exp(student - student_max[:, None])
    stats = jnp.stack(
        [
            teacher_max,
            jnp.sum(teacher_exp, axis=1),
            jnp.sum(teacher_exp * (teacher - student), axis=1),
            student_max,
            jnp.sum(student_exp, axis=1),
        ]
    )
    every = jnp.stack(
        [
            stats,
            to_core(stats),
            send(stats, lambda zl, y, zh, x, core: (zl, y, zh, x ^ 1, core)),
            send(stats, lambda zl, y, zh, x, core: (zl, y, zh, x ^ 1, 1 - core)),
        ]
    )
    teacher_top = jnp.max(every[:, 0], axis=0)
    student_top = jnp.max(every[:, 3], axis=0)
    teacher_shift = jnp.exp(every[:, 0] - teacher_top)
    student_shift = jnp.exp(every[:, 3] - student_top)
    teacher_sum = jnp.sum(every[:, 1] * teacher_shift, axis=0)
    student_sum = jnp.sum(every[:, 4] * student_shift, axis=0)
    weighted = jnp.sum(every[:, 2] * teacher_shift, axis=0)
    divergence = (
        weighted / teacher_sum - (teacher_top + jnp.log(teacher_sum)) + (student_top + jnp.log(student_sum))
    )
    book = zl * 2 + x // 2
    depth_rows = jnp.repeat(depth_cut, FRAMES)
    depth_weight = (book < depth_rows).astype(f32) / depth_rows.astype(f32)
    teacher_factor = teacher_shift[0] / teacher_sum * depth_weight
    student_factor = student_shift[0] / student_sum * depth_weight
    score_grad = (
        student_exp * student_factor[:, None] - teacher_exp * teacher_factor[:, None]
    ).astype(bf16)

    own_kl = (divergence * depth_weight)[None]
    kl = [
        own_kl,
        send(own_kl, lambda zl, y, zh, x, core: (zl, y, zh, x ^ 2, core)),
        send(own_kl, lambda zl, y, zh, x, core: (1 - zl, y, zh, x, core)),
        send(own_kl, lambda zl, y, zh, x, core: (1 - zl, y, zh, x ^ 2, core)),
    ]
    kl = jnp.concatenate(kl)
    kl_terms = jnp.concatenate(
        [lax.dynamic_slice_in_dim(kl, book ^ i, 1, 0) for i in range(C)]
    )

    grad_slots = [score_grad] + [to_zh(score_grad, k) for k in (1, 2, 3)]
    own, other = hidden_grad_parts(index, grad_slots, head_slots)
    other = to_core(other)
    head_grad, *parts = head_grad_parts(hidden, grad_slots)
    for j in (1, 2, 3):
        head_grad = head_grad + to_y(parts[j - 1], -j).astype(f32)
    by_x = own[:2] + other[:2]
    for step in (1, 2, 3):
        part = own[2 * step : 2 * step + 2] + other[2 * step : 2 * step + 2]
        by_x = by_x + to_x(part.astype(bf16), step).astype(f32)

    def home(zl, y, zh, x, core):
        return zl, y, x % 2 * 2 + core, x // 2 * 2 + zh // 2, zh % 2

    by_x = by_x.astype(bf16)
    hidden_grad = send(by_x[0], home).astype(f32) + send(
        by_x[1], lambda zl, y, zh, x, core: home(1 - zl, y, zh, x, core)
    ).astype(f32)
    return (kl_terms, hidden_grad, head_grad)


def solution(mesh):
    return jax.shard_map(
        step,
        mesh=mesh,
        in_specs=(
            P("dp", PLANE),
            P(PLANE),
            P(PLANE, None),
            P("dp", None),
            P("dp", PLANE),
            P("dp"),
        ),
        out_specs=(P(None, "dp"), P("dp", PLANE), P("dp", PLANE)),
        check_vma=False,
    )
```

```python
import jax
import jax.numpy as jnp
from jax import lax
from jax.experimental import pallas as pl
from jax.experimental.pallas import tpu as pltpu
from jax.sharding import PartitionSpec as P

DT = 8192
C = 4
FRAMES = 64
epsilon = 1e-05

ALL = ("group", "dp", "mp")
PLANE = ("group", "mp")


def place(zl, y, zh, x, core):
    return zl * 128 + (y % 4 * 4 + zh % 4) * 8 + x % 4 * 2 + core


def send(value, target):
    pairs = []
    for zl in range(2):
        for y in range(4):
            for zh in range(4):
                for x in range(4):
                    for core in range(2):
                        pairs.append((place(zl, y, zh, x, core), place(*target(zl, y, zh, x, core))))
    return lax.ppermute(value, ALL, pairs)


def to_y(value, step):
    return send(value, lambda zl, y, zh, x, core: (zl, y + step, zh, x, core))


def to_zh(value, step):
    return send(value, lambda zl, y, zh, x, core: (zl, y, zh + step, x, core))


def to_x(value, step):
    return send(value, lambda zl, y, zh, x, core: (zl, y, zh, x + step, core))


def to_zl(value):
    return send(value, lambda zl, y, zh, x, core: (1 - zl, y, zh, x, core))


def to_core(value):
    return send(value, lambda zl, y, zh, x, core: (zl, y, zh, x, 1 - core))


def coordinates(index):
    return index // 128, index // 32 % 4, index // 8 % 4, index // 2 % 4, index % 2


def hidden_block(k, p):
    def spot(i, index_ref):
        _, y, zh, _, core = coordinates(index_ref[0])
        return 0, (y + 8 - p - 2 * core) % 4 * 4 + (zh + k) % 4

    return pl.BlockSpec((128, 256), spot)


def pick_kernel(index_ref, *refs):
    block_refs, out_refs = refs[:6], refs[6:]
    for k in range(3):
        for p in range(2):
            out_refs[k][p] = block_refs[2 * k + p][...]


def picked_blocks(index, hidden):
    return pl.pallas_call(
        pick_kernel,
        grid_spec=pltpu.PrefetchScalarGridSpec(
            num_scalar_prefetch=1,
            grid=(1,),
            in_specs=[hidden_block(k, p) for k in (1, 2, 3) for p in range(2)],
            out_specs=[pl.BlockSpec((2, 128, 256), lambda i, index_ref: (0, 0, 0))] * 3,
        ),
        out_shape=[jax.ShapeDtypeStruct((2, 128, 256), hidden.dtype)] * 3,
        name="pick",
    )(index, *[hidden] * 6)


def split(value):
    high = value.astype(jnp.bfloat16)
    return high, (value - high.astype(jnp.float32)).astype(jnp.bfloat16)


def teacher_kernel(index_ref, hidden_ref, gain_ref, *refs):
    head_refs, out_ref, both_ref, squares_ref = refs[:4], refs[4], refs[5], refs[6]
    rows, depth = hidden_ref.shape

    @pl.when(pl.program_id(0) == 0)
    def _():
        hidden = hidden_ref[...].astype(jnp.float32)
        high, low = split(hidden * gain_ref[...].astype(jnp.float32).reshape(1, depth))
        both_ref[:rows] = high
        both_ref[rows:] = low
        eighth = jnp.full((8, depth), 0.125, jnp.bfloat16)
        squares = sum(
            lax.dot_general(eighth, part, (((1,), (1,)), ((), ())), preferred_element_type=jnp.float32)
            for part in split(hidden * hidden)
        )
        squares_ref[...] = jnp.zeros_like(squares_ref)
        squares_ref[:, :rows] = squares

    for i in range(4):
        scores = jnp.dot(both_ref[...], head_refs[i][...], preferred_element_type=jnp.float32)
        out_ref[i, :rows] = scores[:rows] + scores[rows:]
        out_ref[i, rows:] = squares_ref[...]


def teacher_parts(index, hidden, gain, head, other):
    rows, depth = hidden.shape

    def block(n):
        def spot(i, index_ref):
            zl, _, _, x, core = coordinates(index_ref[0])
            zl = (zl + n) % 2
            return 0, (zl * 4 + (x + 2 * i + n // 2) % 4) * 2 + (core + other) % 2

        return pl.BlockSpec((depth, 512), spot)

    return pl.pallas_call(
        teacher_kernel,
        grid_spec=pltpu.PrefetchScalarGridSpec(
            num_scalar_prefetch=1,
            grid=(2,),
            in_specs=[
                pl.BlockSpec((rows, depth), lambda i, index_ref: (0, 0)),
                pl.BlockSpec((depth,), lambda i, index_ref: (0,)),
                *(block(n) for n in range(4)),
            ],
            out_specs=pl.BlockSpec((4, rows + 8, 512), lambda i, index_ref: (i, 0, 0)),
            scratch_shapes=[pltpu.VMEM((2 * rows, depth), jnp.bfloat16), pltpu.VMEM((8, 512), jnp.float32)],
        ),
        out_shape=jax.ShapeDtypeStruct((8, rows + 8, 512), jnp.float32),
        name="teacher",
    )(index, hidden, gain, head, head, head, head)


ANYWHERE = pl.BlockSpec(memory_space=pl.ANY)


def loads(sources, targets, sems):
    copies = [
        pltpu.make_async_copy(source, target, sems.at[i]) for i, (source, target) in enumerate(zip(sources, targets))
    ]
    for copy in copies:
        copy.start()
    return copies


def student_kernel(index_ref, *refs):
    own_refs, near_refs, far_refs, head_refs = refs[:4], refs[4:7], refs[7:10], refs[10:14]
    first_ref, out_ref, hidden_ref, head_ref, sems = refs[14:]
    core = index_ref[0] % 2
    copies = loads(
        [*head_refs, *near_refs, *far_refs],
        [head_ref.at[j] for j in range(4)]
        + [hidden_ref.at[k, pl.ds(2 * core, 2)] for k in (1, 2, 3)]
        + [hidden_ref.at[k, pl.ds(2 * (1 - core), 2)] for k in (1, 2, 3)],
        sems,
    )
    for p in range(2):
        hidden_ref[0, 2 * core + p] = own_refs[p][...]
        hidden_ref[0, 2 * (1 - core) + p] = own_refs[2 + p][...]
    for copy in copies:
        copy.wait()
    for k in range(4):
        total = None
        for j in range(4):
            term = jnp.dot(hidden_ref[k, j], head_ref[j], preferred_element_type=jnp.float32)
            total = term if total is None else total + term
        if k == 0:
            first_ref[...] = total
        else:
            out_ref[k - 1] = total


def student_parts(index, own, near, far, head_slots):
    def whole(*shape):
        return pl.BlockSpec(shape, lambda i, index_ref: (0,) * len(shape))

    return pl.pallas_call(
        student_kernel,
        grid_spec=pltpu.PrefetchScalarGridSpec(
            num_scalar_prefetch=1,
            grid=(1,),
            in_specs=[hidden_block(0, p) for p in range(4)]
            + [ANYWHERE] * 10,
            out_specs=(whole(128, 512), whole(3, 128, 512), whole(4, 4, 128, 256), whole(4, 256, 512)),
            scratch_shapes=[pltpu.SemaphoreType.DMA((10,))],
        ),
        out_shape=(
            jax.ShapeDtypeStruct((128, 512), jnp.float32),
            jax.ShapeDtypeStruct((3, 128, 512), jnp.float32),
            jax.ShapeDtypeStruct((4, 4, 128, 256), jnp.bfloat16),
            jax.ShapeDtypeStruct((4, 256, 512), jnp.bfloat16),
        ),
        name="student",
    )(index, *[own] * 4, *near, *far, *head_slots)


def head_grad_kernel(states_ref, slots_ref, own_ref, *out_refs):
    for j in range(4):
        total = None
        for k in range(4):
            term = lax.dot_general(
                states_ref[k, j], slots_ref[k], (((0,), (0,)), ((), ())), preferred_element_type=jnp.float32
            )
            total = term if total is None else total + term
        if j == 0:
            own_ref[...] = total
        else:
            out_refs[j - 1][...] = total.astype(jnp.bfloat16)


def head_grad_parts(hidden, slots):
    return pl.pallas_call(
        head_grad_kernel,
        out_shape=(
            jax.ShapeDtypeStruct((256, 512), jnp.float32),
            *[jax.ShapeDtypeStruct((256, 512), jnp.bfloat16)] * 3,
        ),
        name="head_grad",
    )(hidden, slots)


def hidden_grad_kernel(index_ref, *refs):
    grad_refs, head_ref, own_ref, other_ref, slots_ref, sems = refs[:4], *refs[4:]
    zl, y, zh, x, core = coordinates(index_ref[0])
    for copy in loads(grad_refs, [slots_ref.at[k] for k in range(4)], sems):
        copy.wait()
    for j in range(4):
        for m in range(2):
            a = (y + 4 - j) % 4
            for out_ref, side in ((own_ref, core), (other_ref, 1 - core)):
                goal = 2 * m + side
                spot = (a % 2 * 2 + m + 4 - x) % 4 * 2 + (a // 2 + zl) % 2
                out_ref[spot] = lax.dot_general(
                    slots_ref[(zh + 4 - goal) % 4],
                    head_ref[j],
                    (((1,), (1,)), ((), ())),
                    preferred_element_type=jnp.float32,
                )


def hidden_grad_parts(index, grad_slots, head):
    return pl.pallas_call(
        hidden_grad_kernel,
        in_specs=[pl.BlockSpec(memory_space=pltpu.SMEM)]
        + [ANYWHERE] * 4
        + [pl.BlockSpec(memory_space=pltpu.VMEM)],
        out_shape=(
            *[jax.ShapeDtypeStruct((8, 128, 256), jnp.float32)] * 2,
            jax.ShapeDtypeStruct((4, 128, 512), jnp.bfloat16),
        ),
        scratch_shapes=[pltpu.SemaphoreType.DMA((4,))],
        name="hidden_grad",
    )(index, *grad_slots, head)


def step(teacher_hidden, teacher_gain, teacher_head, student_hidden, student_head, depth_cut):
    f32, f16, bf16 = jnp.float32, jnp.float16, jnp.bfloat16
    zl = lax.axis_index("group")
    x = lax.axis_index("mp") // 2
    index = lax.axis_index(ALL).reshape(1)

    halves = picked_blocks(index, student_hidden)
    near = [to_zh(halves[k - 1], k) for k in (1, 2, 3)]
    head_slots = [student_head] + [to_y(student_head, j) for j in (1, 2, 3)]
    far = [to_core(half) for half in near]

    other = teacher_parts(index, teacher_hidden, teacher_gain, teacher_head, 1)
    other = to_core(other)
    parts = teacher_parts(index, teacher_hidden, teacher_gain, teacher_head, 0)
    by_x = parts[:2] + other[:2]
    for step in (1, 2, 3):
        part = parts[2 * step : 2 * step + 2] + other[2 * step : 2 * step + 2]
        by_x = by_x + to_x(part.astype(f16), step).astype(f32)
    teacher = by_x[0] + to_zl(by_x[1].astype(f16)).astype(f32)

    student, parts, hidden, head = student_parts(index, student_hidden, near, far, head_slots)
    parts = parts.astype(f16)
    for k in (1, 2, 3):
        student = student + to_zh(parts[k - 1], -k).astype(f32)

    row_scale = lax.rsqrt(teacher[128, :128] * (8 / DT) + epsilon)
    teacher = teacher[:128] * row_scale[:, None]

    teacher_max = jnp.max(teacher, axis=1)
    student_max = jnp.max(student, axis=1)
    teacher_exp = jnp.exp(teacher - teacher_max[:, None])
    student_exp = jnp.exp(student - student_max[:, None])
    stats = jnp.stack(
        [
            teacher_max,
            jnp.sum(teacher_exp, axis=1),
            jnp.sum(teacher_exp * (teacher - student), axis=1),
            student_max,
            jnp.sum(student_exp, axis=1),
        ]
    )
    every = jnp.stack(
        [
            stats,
            to_core(stats),
            send(stats, lambda zl, y, zh, x, core: (zl, y, zh, x ^ 1, core)),
            send(stats, lambda zl, y, zh, x, core: (zl, y, zh, x ^ 1, 1 - core)),
        ]
    )
    teacher_top = jnp.max(every[:, 0], axis=0)
    student_top = jnp.max(every[:, 3], axis=0)
    teacher_shift = jnp.exp(every[:, 0] - teacher_top)
    student_shift = jnp.exp(every[:, 3] - student_top)
    teacher_sum = jnp.sum(every[:, 1] * teacher_shift, axis=0)
    student_sum = jnp.sum(every[:, 4] * student_shift, axis=0)
    weighted = jnp.sum(every[:, 2] * teacher_shift, axis=0)
    divergence = (
        weighted / teacher_sum - (teacher_top + jnp.log(teacher_sum)) + (student_top + jnp.log(student_sum))
    )
    book = zl * 2 + x // 2
    depth_rows = jnp.repeat(depth_cut, FRAMES)
    depth_weight = (book < depth_rows).astype(f32) / depth_rows.astype(f32)
    teacher_factor = teacher_shift[0] / teacher_sum * depth_weight
    student_factor = student_shift[0] / student_sum * depth_weight
    score_grad = (
        student_exp * student_factor[:, None] - teacher_exp * teacher_factor[:, None]
    ).astype(bf16)

    own_kl = (divergence * depth_weight)[None]
    kl = [
        own_kl,
        send(own_kl, lambda zl, y, zh, x, core: (zl, y, zh, x ^ 2, core)),
        send(own_kl, lambda zl, y, zh, x, core: (1 - zl, y, zh, x, core)),
        send(own_kl, lambda zl, y, zh, x, core: (1 - zl, y, zh, x ^ 2, core)),
    ]
    kl = jnp.concatenate(kl)
    kl_terms = jnp.concatenate(
        [lax.dynamic_slice_in_dim(kl, book ^ i, 1, 0) for i in range(C)]
    )

    grad_slots = [score_grad] + [to_zh(score_grad, k) for k in (1, 2, 3)]
    own, other, slots = hidden_grad_parts(index, grad_slots, head)
    other = to_core(other)
    head_grad, *parts = head_grad_parts(hidden, slots)
    for j in (1, 2, 3):
        head_grad = head_grad + to_y(parts[j - 1], -j).astype(f32)
    by_x = own[:2] + other[:2]
    for step in (1, 2, 3):
        part = own[2 * step : 2 * step + 2] + other[2 * step : 2 * step + 2]
        by_x = by_x + to_x(part.astype(bf16), step).astype(f32)

    def home(zl, y, zh, x, core):
        return zl, y, x % 2 * 2 + core, x // 2 * 2 + zh // 2, zh % 2

    by_x = by_x.astype(bf16)
    hidden_grad = send(by_x[0], home).astype(f32) + send(
        by_x[1], lambda zl, y, zh, x, core: home(1 - zl, y, zh, x, core)
    ).astype(f32)
    return (kl_terms, hidden_grad, head_grad)


def solution(mesh):
    return jax.shard_map(
        step,
        mesh=mesh,
        in_specs=(
            P("dp", PLANE),
            P(PLANE),
            P(PLANE, None),
            P("dp", None),
            P("dp", PLANE),
            P("dp"),
        ),
        out_specs=(P(None, "dp"), P("dp", PLANE), P("dp", PLANE)),
        check_vma=False,
    )
```

```python
import jax
import jax.numpy as jnp
from jax import lax
from jax.experimental import pallas as pl
from jax.experimental.pallas import tpu as pltpu
from jax.sharding import PartitionSpec as P

DT = 8192
C = 4
FRAMES = 64
epsilon = 1e-05

ALL = ("group", "dp", "mp")
PLANE = ("group", "mp")


def place(zl, y, zh, x, core):
    return zl * 128 + (y % 4 * 4 + zh % 4) * 8 + x % 4 * 2 + core


def send(value, target):
    pairs = []
    for zl in range(2):
        for y in range(4):
            for zh in range(4):
                for x in range(4):
                    for core in range(2):
                        pairs.append((place(zl, y, zh, x, core), place(*target(zl, y, zh, x, core))))
    return lax.ppermute(value, ALL, pairs)


def to_y(value, step):
    return send(value, lambda zl, y, zh, x, core: (zl, y + step, zh, x, core))


def to_zh(value, step):
    return send(value, lambda zl, y, zh, x, core: (zl, y, zh + step, x, core))


def to_x(value, step):
    return send(value, lambda zl, y, zh, x, core: (zl, y, zh, x + step, core))


def to_zl(value):
    return send(value, lambda zl, y, zh, x, core: (1 - zl, y, zh, x, core))


def to_core(value):
    return send(value, lambda zl, y, zh, x, core: (zl, y, zh, x, 1 - core))


def coordinates(index):
    return index // 128, index // 32 % 4, index // 8 % 4, index // 2 % 4, index % 2


def hidden_block(k, p):
    def spot(i, index_ref):
        _, y, zh, _, core = coordinates(index_ref[0])
        return 0, (y + 8 - p - 2 * core) % 4 * 4 + (zh + k) % 4

    return pl.BlockSpec((128, 256), spot)


def pick_kernel(index_ref, *refs):
    block_refs, out_refs = refs[:6], refs[6:]
    for k in range(3):
        for p in range(2):
            out_refs[k][p] = block_refs[2 * k + p][...]


def picked_blocks(index, hidden):
    return pl.pallas_call(
        pick_kernel,
        grid_spec=pltpu.PrefetchScalarGridSpec(
            num_scalar_prefetch=1,
            grid=(1,),
            in_specs=[hidden_block(k, p) for k in (1, 2, 3) for p in range(2)],
            out_specs=[pl.BlockSpec((2, 128, 256), lambda i, index_ref: (0, 0, 0))] * 3,
        ),
        out_shape=[jax.ShapeDtypeStruct((2, 128, 256), hidden.dtype)] * 3,
        name="pick",
    )(index, *[hidden] * 6)


def split(value):
    high = value.astype(jnp.bfloat16)
    return high, (value - high.astype(jnp.float32)).astype(jnp.bfloat16)


def teacher_kernel(index_ref, hidden_ref, gain_ref, *refs):
    head_refs, out_ref, both_ref, squares_ref = refs[:4], refs[4], refs[5], refs[6]
    rows, depth = hidden_ref.shape

    @pl.when(pl.program_id(0) == 0)
    def _():
        hidden = hidden_ref[...].astype(jnp.float32)
        high, low = split(hidden * gain_ref[...].astype(jnp.float32).reshape(1, depth))
        both_ref[:rows] = high
        both_ref[rows:] = low
        eighth = jnp.full((8, depth), 0.125, jnp.bfloat16)
        squares = sum(
            lax.dot_general(eighth, part, (((1,), (1,)), ((), ())), preferred_element_type=jnp.float32)
            for part in split(hidden * hidden)
        )
        squares_ref[...] = jnp.zeros_like(squares_ref)
        squares_ref[:, :rows] = squares

    for i in range(4):
        scores = jnp.dot(both_ref[...], head_refs[i][...], preferred_element_type=jnp.float32)
        out_ref[i, :rows] = scores[:rows] + scores[rows:]
        out_ref[i, rows:] = squares_ref[...]


def teacher_parts(index, hidden, gain, head, other):
    rows, depth = hidden.shape

    def block(n):
        def spot(i, index_ref):
            zl, _, _, x, core = coordinates(index_ref[0])
            zl = (zl + n) % 2
            return 0, (zl * 4 + (x + 2 * i + n // 2) % 4) * 2 + (core + other) % 2

        return pl.BlockSpec((depth, 512), spot)

    return pl.pallas_call(
        teacher_kernel,
        grid_spec=pltpu.PrefetchScalarGridSpec(
            num_scalar_prefetch=1,
            grid=(2,),
            in_specs=[
                pl.BlockSpec((rows, depth), lambda i, index_ref: (0, 0)),
                pl.BlockSpec((depth,), lambda i, index_ref: (0,)),
                *(block(n) for n in range(4)),
            ],
            out_specs=pl.BlockSpec((4, rows + 8, 512), lambda i, index_ref: (i, 0, 0)),
            scratch_shapes=[pltpu.VMEM((2 * rows, depth), jnp.bfloat16), pltpu.VMEM((8, 512), jnp.float32)],
        ),
        out_shape=jax.ShapeDtypeStruct((8, rows + 8, 512), jnp.float32),
        name="teacher",
    )(index, hidden, gain, head, head, head, head)


ANYWHERE = pl.BlockSpec(memory_space=pl.ANY)


def loads(sources, targets, sems):
    copies = [
        pltpu.make_async_copy(source, target, sems.at[i]) for i, (source, target) in enumerate(zip(sources, targets))
    ]
    for copy in copies:
        copy.start()
    return copies


def student_kernel(index_ref, *refs):
    own_refs, near_refs, far_refs, head_refs = refs[:4], refs[4:7], refs[7:10], refs[10:14]
    first_ref, out_ref, hidden_ref, head_ref, sems = refs[14:]
    core = index_ref[0] % 2

    def spot(k, side, p):
        return pl.ds(128 * k, 128), pl.ds(pl.multiple_of((2 * side + p) * 256, 256), 256)

    copies = loads(
        [*head_refs]
        + [near_refs[k - 1].at[p] for k in (1, 2, 3) for p in range(2)]
        + [far_refs[k - 1].at[p] for k in (1, 2, 3) for p in range(2)],
        [head_ref.at[pl.ds(256 * j, 256)] for j in range(4)]
        + [hidden_ref.at[spot(k, core, p)] for k in (1, 2, 3) for p in range(2)]
        + [hidden_ref.at[spot(k, 1 - core, p)] for k in (1, 2, 3) for p in range(2)],
        sems,
    )
    for p in range(2):
        hidden_ref[spot(0, core, p)] = own_refs[p][...]
        hidden_ref[spot(0, 1 - core, p)] = own_refs[2 + p][...]
    for copy in copies:
        copy.wait()
    scores = jnp.dot(hidden_ref[...], head_ref[...], preferred_element_type=jnp.float32)
    first_ref[...] = scores[:128]
    for k in (1, 2, 3):
        out_ref[k - 1] = scores[128 * k : 128 * (k + 1)]


def student_parts(index, own, near, far, head_slots):
    def whole(*shape):
        return pl.BlockSpec(shape, lambda i, index_ref: (0,) * len(shape))

    return pl.pallas_call(
        student_kernel,
        grid_spec=pltpu.PrefetchScalarGridSpec(
            num_scalar_prefetch=1,
            grid=(1,),
            in_specs=[hidden_block(0, p) for p in range(4)]
            + [ANYWHERE] * 10,
            out_specs=(whole(128, 512), whole(3, 128, 512), whole(512, 1024), whole(1024, 512)),
            scratch_shapes=[pltpu.SemaphoreType.DMA((16,))],
        ),
        out_shape=(
            jax.ShapeDtypeStruct((128, 512), jnp.float32),
            jax.ShapeDtypeStruct((3, 128, 512), jnp.float32),
            jax.ShapeDtypeStruct((512, 1024), jnp.bfloat16),
            jax.ShapeDtypeStruct((1024, 512), jnp.bfloat16),
        ),
        name="student",
    )(index, *[own] * 4, *near, *far, *head_slots)


def head_grad_kernel(hidden_ref, *refs):
    grad_refs, own_ref, out_refs, slots_ref = refs[:4], refs[4], refs[5:8], refs[8]
    for k in range(4):
        slots_ref[128 * k : 128 * (k + 1)] = grad_refs[k][...]
    for j in (1, 2, 3, 0):
        total = lax.dot_general(
            hidden_ref[:, 256 * j : 256 * (j + 1)],
            slots_ref[...],
            (((0,), (0,)), ((), ())),
            preferred_element_type=jnp.float32,
        )
        if j == 0:
            own_ref[...] = total
        else:
            out_refs[j - 1][...] = total.astype(jnp.bfloat16)


def head_grad_parts(hidden, grad_slots):
    return pl.pallas_call(
        head_grad_kernel,
        out_shape=(
            jax.ShapeDtypeStruct((256, 512), jnp.float32),
            *[jax.ShapeDtypeStruct((256, 512), jnp.bfloat16)] * 3,
        ),
        scratch_shapes=[pltpu.VMEM((512, 512), jnp.bfloat16)],
        name="head_grad",
    )(hidden, *grad_slots)


def hidden_grad_kernel(index_ref, *refs):
    grad_refs, head_ref, own_ref, other_ref, slots_ref, sorted_ref = refs[:4], *refs[4:]
    zl, y, zh, x, core = coordinates(index_ref[0])
    for k in range(4):
        slots_ref[k] = grad_refs[k][...]
    goals = [2 * m + side for side in (core, 1 - core) for m in range(2)]
    for i, goal in enumerate(goals):
        sorted_ref[128 * i : 128 * (i + 1)] = slots_ref[(zh + 4 - goal) % 4]
    for j in range(4):
        a = (y + 4 - j) % 4
        terms = lax.dot_general(
            sorted_ref[...],
            head_ref[256 * j : 256 * (j + 1)],
            (((1,), (1,)), ((), ())),
            preferred_element_type=jnp.float32,
        )
        for m in range(2):
            spot = (a % 2 * 2 + m + 4 - x) % 4 * 2 + (a // 2 + zl) % 2
            own_ref[spot] = terms[128 * m : 128 * (m + 1)]
            other_ref[spot] = terms[128 * (2 + m) : 128 * (3 + m)]


def hidden_grad_parts(index, grad_slots, head):
    return pl.pallas_call(
        hidden_grad_kernel,
        in_specs=[pl.BlockSpec(memory_space=pltpu.SMEM)] + [pl.BlockSpec(memory_space=pltpu.VMEM)] * 5,
        out_shape=(jax.ShapeDtypeStruct((8, 128, 256), jnp.float32),) * 2,
        scratch_shapes=[pltpu.VMEM((4, 128, 512), jnp.bfloat16), pltpu.VMEM((512, 512), jnp.bfloat16)],
        name="hidden_grad",
    )(index, *grad_slots, head)


def step(teacher_hidden, teacher_gain, teacher_head, student_hidden, student_head, depth_cut):
    f32, f16, bf16 = jnp.float32, jnp.float16, jnp.bfloat16
    zl = lax.axis_index("group")
    x = lax.axis_index("mp") // 2
    index = lax.axis_index(ALL).reshape(1)

    halves = picked_blocks(index, student_hidden)
    near = [to_zh(halves[k - 1], k) for k in (1, 2, 3)]
    head_slots = [student_head] + [to_y(student_head, j) for j in (1, 2, 3)]
    far = [to_core(half) for half in near]

    other = teacher_parts(index, teacher_hidden, teacher_gain, teacher_head, 1)
    other = to_core(other)
    parts = teacher_parts(index, teacher_hidden, teacher_gain, teacher_head, 0)
    by_x = parts[:2] + other[:2]
    for step in (1, 2, 3):
        part = parts[2 * step : 2 * step + 2] + other[2 * step : 2 * step + 2]
        by_x = by_x + to_x(part.astype(f16), step).astype(f32)
    teacher = by_x[0] + to_zl(by_x[1].astype(f16)).astype(f32)

    student, parts, hidden, head = student_parts(index, student_hidden, near, far, head_slots)
    parts = parts.astype(f16)
    for k in (1, 2, 3):
        student = student + to_zh(parts[k - 1], -k).astype(f32)

    row_scale = lax.rsqrt(teacher[128, :128] * (8 / DT) + epsilon)
    teacher = teacher[:128] * row_scale[:, None]

    teacher_max = jnp.max(teacher, axis=1)
    student_max = jnp.max(student, axis=1)
    teacher_exp = jnp.exp(teacher - teacher_max[:, None])
    student_exp = jnp.exp(student - student_max[:, None])
    stats = jnp.stack(
        [
            teacher_max,
            jnp.sum(teacher_exp, axis=1),
            jnp.sum(teacher_exp * (teacher - student), axis=1),
            student_max,
            jnp.sum(student_exp, axis=1),
        ]
    )
    every = jnp.stack(
        [
            stats,
            to_core(stats),
            send(stats, lambda zl, y, zh, x, core: (zl, y, zh, x ^ 1, core)),
            send(stats, lambda zl, y, zh, x, core: (zl, y, zh, x ^ 1, 1 - core)),
        ]
    )
    teacher_top = jnp.max(every[:, 0], axis=0)
    student_top = jnp.max(every[:, 3], axis=0)
    teacher_shift = jnp.exp(every[:, 0] - teacher_top)
    student_shift = jnp.exp(every[:, 3] - student_top)
    teacher_sum = jnp.sum(every[:, 1] * teacher_shift, axis=0)
    student_sum = jnp.sum(every[:, 4] * student_shift, axis=0)
    weighted = jnp.sum(every[:, 2] * teacher_shift, axis=0)
    divergence = (
        weighted / teacher_sum - (teacher_top + jnp.log(teacher_sum)) + (student_top + jnp.log(student_sum))
    )
    book = zl * 2 + x // 2
    depth_rows = jnp.repeat(depth_cut, FRAMES)
    depth_weight = (book < depth_rows).astype(f32) / depth_rows.astype(f32)
    teacher_factor = teacher_shift[0] / teacher_sum * depth_weight
    student_factor = student_shift[0] / student_sum * depth_weight
    score_grad = (
        student_exp * student_factor[:, None] - teacher_exp * teacher_factor[:, None]
    ).astype(bf16)

    own_kl = (divergence * depth_weight)[None]
    kl = [
        own_kl,
        send(own_kl, lambda zl, y, zh, x, core: (zl, y, zh, x ^ 2, core)),
        send(own_kl, lambda zl, y, zh, x, core: (1 - zl, y, zh, x, core)),
        send(own_kl, lambda zl, y, zh, x, core: (1 - zl, y, zh, x ^ 2, core)),
    ]
    kl = jnp.concatenate(kl)
    kl_terms = jnp.concatenate(
        [lax.dynamic_slice_in_dim(kl, book ^ i, 1, 0) for i in range(C)]
    )

    grad_slots = [score_grad] + [to_zh(score_grad, k) for k in (1, 2, 3)]
    own, other = hidden_grad_parts(index, grad_slots, head)
    other = to_core(other)
    head_grad, *parts = head_grad_parts(hidden, grad_slots)
    for j in (1, 2, 3):
        head_grad = head_grad + to_y(parts[j - 1], -j).astype(f32)
    by_x = own[:2] + other[:2]
    for step in (1, 2, 3):
        part = own[2 * step : 2 * step + 2] + other[2 * step : 2 * step + 2]
        by_x = by_x + to_x(part.astype(bf16), step).astype(f32)

    def home(zl, y, zh, x, core):
        return zl, y, x % 2 * 2 + core, x // 2 * 2 + zh // 2, zh % 2

    by_x = by_x.astype(bf16)
    hidden_grad = send(by_x[0], home).astype(f32) + send(
        by_x[1], lambda zl, y, zh, x, core: home(1 - zl, y, zh, x, core)
    ).astype(f32)
    return (kl_terms, hidden_grad, head_grad)


def solution(mesh):
    return jax.shard_map(
        step,
        mesh=mesh,
        in_specs=(
            P("dp", PLANE),
            P(PLANE),
            P(PLANE, None),
            P("dp", None),
            P("dp", PLANE),
            P("dp"),
        ),
        out_specs=(P(None, "dp"), P("dp", PLANE), P("dp", PLANE)),
        check_vma=False,
    )
```

```python
import jax
import jax.numpy as jnp
from jax import lax
from jax.experimental import pallas as pl
from jax.experimental.pallas import tpu as pltpu
from jax.sharding import PartitionSpec as P

DT = 8192
C = 4
FRAMES = 64
epsilon = 1e-05

ALL = ("group", "dp", "mp")
PLANE = ("group", "mp")


def place(zl, y, zh, x, core):
    return zl * 128 + (y % 4 * 4 + zh % 4) * 8 + x % 4 * 2 + core


def send(value, target):
    pairs = []
    for zl in range(2):
        for y in range(4):
            for zh in range(4):
                for x in range(4):
                    for core in range(2):
                        pairs.append((place(zl, y, zh, x, core), place(*target(zl, y, zh, x, core))))
    return lax.ppermute(value, ALL, pairs)


def to_y(value, step):
    return send(value, lambda zl, y, zh, x, core: (zl, y + step, zh, x, core))


def to_zh(value, step):
    return send(value, lambda zl, y, zh, x, core: (zl, y, zh + step, x, core))


def to_x(value, step):
    return send(value, lambda zl, y, zh, x, core: (zl, y, zh, x + step, core))


def to_zl(value):
    return send(value, lambda zl, y, zh, x, core: (1 - zl, y, zh, x, core))


def to_core(value):
    return send(value, lambda zl, y, zh, x, core: (zl, y, zh, x, 1 - core))


def coordinates(index):
    return index // 128, index // 32 % 4, index // 8 % 4, index // 2 % 4, index % 2


def hidden_block(k, p):
    def spot(i, index_ref):
        _, y, zh, _, core = coordinates(index_ref[0])
        return 0, (y + 8 - p - 2 * core) % 4 * 4 + (zh + k) % 4

    return pl.BlockSpec((128, 256), spot)


def pick_kernel(index_ref, *refs):
    block_refs, out_refs = refs[:6], refs[6:]
    for k in range(3):
        for p in range(2):
            out_refs[k][p] = block_refs[2 * k + p][...]


def picked_blocks(index, hidden):
    return pl.pallas_call(
        pick_kernel,
        grid_spec=pltpu.PrefetchScalarGridSpec(
            num_scalar_prefetch=1,
            grid=(1,),
            in_specs=[hidden_block(k, p) for k in (1, 2, 3) for p in range(2)],
            out_specs=[pl.BlockSpec((2, 128, 256), lambda i, index_ref: (0, 0, 0))] * 3,
        ),
        out_shape=[jax.ShapeDtypeStruct((2, 128, 256), hidden.dtype)] * 3,
        name="pick",
    )(index, *[hidden] * 6)


def split(value):
    high = value.astype(jnp.bfloat16)
    return high, (value - high.astype(jnp.float32)).astype(jnp.bfloat16)


def teacher_kernel(index_ref, hidden_ref, gain_ref, *refs):
    head_refs, out_ref, both_ref, squares_ref = refs[:4], refs[4], refs[5], refs[6]
    rows, depth = hidden_ref.shape

    @pl.when(pl.program_id(0) == 0)
    def _():
        hidden = hidden_ref[...].astype(jnp.float32)
        high, low = split(hidden * gain_ref[...].astype(jnp.float32).reshape(1, depth))
        both_ref[:rows] = high
        both_ref[rows:] = low
        eighth = jnp.full((8, depth), 0.125, jnp.bfloat16)
        squares = sum(
            lax.dot_general(eighth, part, (((1,), (1,)), ((), ())), preferred_element_type=jnp.float32)
            for part in split(hidden * hidden)
        )
        squares_ref[...] = jnp.zeros_like(squares_ref)
        squares_ref[:, :rows] = squares

    for i in range(4):
        scores = jnp.dot(both_ref[...], head_refs[i][...], preferred_element_type=jnp.float32)
        out_ref[i, :rows] = scores[:rows] + scores[rows:]
        out_ref[i, rows:] = squares_ref[...]


def teacher_parts(index, hidden, gain, head, other):
    rows, depth = hidden.shape

    def block(n):
        def spot(i, index_ref):
            zl, _, _, x, core = coordinates(index_ref[0])
            zl = (zl + n) % 2
            return 0, (zl * 4 + (x + 2 * i + n // 2) % 4) * 2 + (core + other) % 2

        return pl.BlockSpec((depth, 512), spot)

    return pl.pallas_call(
        teacher_kernel,
        grid_spec=pltpu.PrefetchScalarGridSpec(
            num_scalar_prefetch=1,
            grid=(2,),
            in_specs=[
                pl.BlockSpec((rows, depth), lambda i, index_ref: (0, 0)),
                pl.BlockSpec((depth,), lambda i, index_ref: (0,)),
                *(block(n) for n in range(4)),
            ],
            out_specs=pl.BlockSpec((4, rows + 8, 512), lambda i, index_ref: (i, 0, 0)),
            scratch_shapes=[pltpu.VMEM((2 * rows, depth), jnp.bfloat16), pltpu.VMEM((8, 512), jnp.float32)],
        ),
        out_shape=jax.ShapeDtypeStruct((8, rows + 8, 512), jnp.float32),
        name="teacher",
    )(index, hidden, gain, head, head, head, head)


ANYWHERE = pl.BlockSpec(memory_space=pl.ANY)


def loads(sources, targets, sems):
    copies = [
        pltpu.make_async_copy(source, target, sems.at[i]) for i, (source, target) in enumerate(zip(sources, targets))
    ]
    for copy in copies:
        copy.start()
    return copies


def student_kernel(index_ref, *refs):
    own_refs, near_refs, far_refs, head_refs = refs[:4], refs[4:7], refs[7:10], refs[10:14]
    first_ref, out_ref, hidden_out, head_out, hidden_ref, head_ref, sems = refs[14:]
    core = index_ref[0] % 2

    def spot(k, side, p):
        return pl.ds(128 * k, 128), pl.ds(pl.multiple_of((2 * side + p) * 256, 256), 256)

    copies = loads(
        [*head_refs]
        + [near_refs[k - 1].at[p] for k in (1, 2, 3) for p in range(2)]
        + [far_refs[k - 1].at[p] for k in (1, 2, 3) for p in range(2)],
        [head_ref.at[pl.ds(256 * j, 256)] for j in range(4)]
        + [hidden_ref.at[spot(k, core, p)] for k in (1, 2, 3) for p in range(2)]
        + [hidden_ref.at[spot(k, 1 - core, p)] for k in (1, 2, 3) for p in range(2)],
        sems,
    )
    for p in range(2):
        hidden_ref[spot(0, core, p)] = own_refs[p][...]
        hidden_ref[spot(0, 1 - core, p)] = own_refs[2 + p][...]
    for copy in copies:
        copy.wait()
    copies = loads([hidden_ref, head_ref], [hidden_out, head_out], sems)
    scores = jnp.dot(hidden_ref[...], head_ref[...], preferred_element_type=jnp.float32)
    first_ref[...] = scores[:128]
    for k in (1, 2, 3):
        out_ref[k - 1] = scores[128 * k : 128 * (k + 1)]
    for copy in copies:
        copy.wait()


def student_parts(index, own, near, far, head_slots):
    def whole(*shape):
        return pl.BlockSpec(shape, lambda i, index_ref: (0,) * len(shape))

    return pl.pallas_call(
        student_kernel,
        grid_spec=pltpu.PrefetchScalarGridSpec(
            num_scalar_prefetch=1,
            grid=(1,),
            in_specs=[hidden_block(0, p) for p in range(4)]
            + [ANYWHERE] * 10,
            out_specs=(whole(128, 512), whole(3, 128, 512), ANYWHERE, ANYWHERE),
            scratch_shapes=[
                pltpu.VMEM((512, 1024), jnp.bfloat16),
                pltpu.VMEM((1024, 512), jnp.bfloat16),
                pltpu.SemaphoreType.DMA((16,)),
            ],
        ),
        out_shape=(
            jax.ShapeDtypeStruct((128, 512), jnp.float32),
            jax.ShapeDtypeStruct((3, 128, 512), jnp.float32),
            jax.ShapeDtypeStruct((512, 1024), jnp.bfloat16),
            jax.ShapeDtypeStruct((1024, 512), jnp.bfloat16),
        ),
        name="student",
    )(index, *[own] * 4, *near, *far, *head_slots)


def head_grad_kernel(hidden_hbm, *refs):
    grad_refs, out_refs = refs[:4], refs[4:8]
    slots_ref, hidden_ref, own_ref, other_ref, in_sems, out_sems = refs[8:]
    order = (1, 2, 3, 0)
    copies = loads(
        [hidden_hbm.at[:, pl.ds(256 * j, 256)] for j in order], [hidden_ref.at[i] for i in range(4)], in_sems
    )
    for k in range(4):
        slots_ref[128 * k : 128 * (k + 1)] = grad_refs[k][...]
    results = []
    for i, j in enumerate(order):
        copies[i].wait()
        total = lax.dot_general(
            hidden_ref[i], slots_ref[...], (((0,), (0,)), ((), ())), preferred_element_type=jnp.float32
        )
        if j == 0:
            own_ref[...] = total
            result = pltpu.make_async_copy(own_ref, out_refs[0], out_sems.at[0])
        else:
            other_ref[j - 1] = total.astype(jnp.bfloat16)
            result = pltpu.make_async_copy(other_ref.at[j - 1], out_refs[j], out_sems.at[j])
        result.start()
        results.append(result)
    for result in results:
        result.wait()


def head_grad_parts(hidden, grad_slots):
    return pl.pallas_call(
        head_grad_kernel,
        in_specs=[ANYWHERE] + [pl.BlockSpec(memory_space=pltpu.VMEM)] * 4,
        out_specs=[ANYWHERE] * 4,
        out_shape=(
            jax.ShapeDtypeStruct((256, 512), jnp.float32),
            *[jax.ShapeDtypeStruct((256, 512), jnp.bfloat16)] * 3,
        ),
        scratch_shapes=[
            pltpu.VMEM((512, 512), jnp.bfloat16),
            pltpu.VMEM((4, 512, 256), jnp.bfloat16),
            pltpu.VMEM((256, 512), jnp.float32),
            pltpu.VMEM((3, 256, 512), jnp.bfloat16),
            pltpu.SemaphoreType.DMA((4,)),
            pltpu.SemaphoreType.DMA((4,)),
        ],
        name="head_grad",
    )(hidden, *grad_slots)


def hidden_grad_kernel(index_ref, *refs):
    grad_refs, head_hbm, own_out, other_out = refs[:4], *refs[4:7]
    slots_ref, sorted_ref, head_ref, own_ref, other_ref, in_sems, out_sems = refs[7:]
    zl, y, zh, x, core = coordinates(index_ref[0])
    copies = loads(
        [head_hbm.at[pl.ds(256 * j, 256)] for j in range(4)], [head_ref.at[j] for j in range(4)], in_sems
    )
    for k in range(4):
        slots_ref[k] = grad_refs[k][...]
    goals = [2 * m + side for side in (core, 1 - core) for m in range(2)]
    for i, goal in enumerate(goals):
        sorted_ref[128 * i : 128 * (i + 1)] = slots_ref[(zh + 4 - goal) % 4]
    results = []
    for j in range(4):
        a = (y + 4 - j) % 4
        copies[j].wait()
        terms = lax.dot_general(
            sorted_ref[...], head_ref[j], (((1,), (1,)), ((), ())), preferred_element_type=jnp.float32
        )
        for m in range(2):
            own_ref[j, m] = terms[128 * m : 128 * (m + 1)]
            other_ref[j, m] = terms[128 * (2 + m) : 128 * (3 + m)]
            spot = (a % 2 * 2 + m + 4 - x) % 4 * 2 + (a // 2 + zl) % 2
            for n, (part, out) in enumerate(((own_ref, own_out), (other_ref, other_out))):
                result = pltpu.make_async_copy(part.at[j, m], out.at[spot], out_sems.at[4 * j + 2 * m + n])
                result.start()
                results.append(result)
    for result in results:
        result.wait()


def hidden_grad_parts(index, grad_slots, head):
    return pl.pallas_call(
        hidden_grad_kernel,
        in_specs=[pl.BlockSpec(memory_space=pltpu.SMEM)]
        + [pl.BlockSpec(memory_space=pltpu.VMEM)] * 4
        + [ANYWHERE],
        out_specs=[ANYWHERE] * 2,
        out_shape=(jax.ShapeDtypeStruct((8, 128, 256), jnp.float32),) * 2,
        scratch_shapes=[
            pltpu.VMEM((4, 128, 512), jnp.bfloat16),
            pltpu.VMEM((512, 512), jnp.bfloat16),
            pltpu.VMEM((4, 256, 512), jnp.bfloat16),
            pltpu.VMEM((4, 2, 128, 256), jnp.float32),
            pltpu.VMEM((4, 2, 128, 256), jnp.float32),
            pltpu.SemaphoreType.DMA((4,)),
            pltpu.SemaphoreType.DMA((16,)),
        ],
        name="hidden_grad",
    )(index, *grad_slots, head)


def step(teacher_hidden, teacher_gain, teacher_head, student_hidden, student_head, depth_cut):
    f32, f16, bf16 = jnp.float32, jnp.float16, jnp.bfloat16
    zl = lax.axis_index("group")
    x = lax.axis_index("mp") // 2
    index = lax.axis_index(ALL).reshape(1)

    halves = picked_blocks(index, student_hidden)
    near = [to_zh(halves[k - 1], k) for k in (1, 2, 3)]
    head_slots = [student_head] + [to_y(student_head, j) for j in (1, 2, 3)]
    far = [to_core(half) for half in near]

    other = teacher_parts(index, teacher_hidden, teacher_gain, teacher_head, 1)
    other = to_core(other)
    parts = teacher_parts(index, teacher_hidden, teacher_gain, teacher_head, 0)
    by_x = parts[:2] + other[:2]
    for step in (1, 2, 3):
        part = parts[2 * step : 2 * step + 2] + other[2 * step : 2 * step + 2]
        by_x = by_x + to_x(part.astype(f16), step).astype(f32)
    teacher = by_x[0] + to_zl(by_x[1].astype(f16)).astype(f32)

    student, parts, hidden, head = student_parts(index, student_hidden, near, far, head_slots)
    parts = parts.astype(f16)
    for k in (1, 2, 3):
        student = student + to_zh(parts[k - 1], -k).astype(f32)

    row_scale = lax.rsqrt(teacher[128, :128] * (8 / DT) + epsilon)
    teacher = teacher[:128] * row_scale[:, None]

    teacher_max = jnp.max(teacher, axis=1)
    student_max = jnp.max(student, axis=1)
    teacher_exp = jnp.exp(teacher - teacher_max[:, None])
    student_exp = jnp.exp(student - student_max[:, None])
    stats = jnp.stack(
        [
            teacher_max,
            jnp.sum(teacher_exp, axis=1),
            jnp.sum(teacher_exp * (teacher - student), axis=1),
            student_max,
            jnp.sum(student_exp, axis=1),
        ]
    )
    every = jnp.stack(
        [
            stats,
            to_core(stats),
            send(stats, lambda zl, y, zh, x, core: (zl, y, zh, x ^ 1, core)),
            send(stats, lambda zl, y, zh, x, core: (zl, y, zh, x ^ 1, 1 - core)),
        ]
    )
    teacher_top = jnp.max(every[:, 0], axis=0)
    student_top = jnp.max(every[:, 3], axis=0)
    teacher_shift = jnp.exp(every[:, 0] - teacher_top)
    student_shift = jnp.exp(every[:, 3] - student_top)
    teacher_sum = jnp.sum(every[:, 1] * teacher_shift, axis=0)
    student_sum = jnp.sum(every[:, 4] * student_shift, axis=0)
    weighted = jnp.sum(every[:, 2] * teacher_shift, axis=0)
    divergence = (
        weighted / teacher_sum - (teacher_top + jnp.log(teacher_sum)) + (student_top + jnp.log(student_sum))
    )
    book = zl * 2 + x // 2
    depth_rows = jnp.repeat(depth_cut, FRAMES)
    depth_weight = (book < depth_rows).astype(f32) / depth_rows.astype(f32)
    teacher_factor = teacher_shift[0] / teacher_sum * depth_weight
    student_factor = student_shift[0] / student_sum * depth_weight
    score_grad = (
        student_exp * student_factor[:, None] - teacher_exp * teacher_factor[:, None]
    ).astype(bf16)

    own_kl = (divergence * depth_weight)[None]
    kl = [
        own_kl,
        send(own_kl, lambda zl, y, zh, x, core: (zl, y, zh, x ^ 2, core)),
        send(own_kl, lambda zl, y, zh, x, core: (1 - zl, y, zh, x, core)),
        send(own_kl, lambda zl, y, zh, x, core: (1 - zl, y, zh, x ^ 2, core)),
    ]
    kl = jnp.concatenate(kl)
    kl_terms = jnp.concatenate(
        [lax.dynamic_slice_in_dim(kl, book ^ i, 1, 0) for i in range(C)]
    )

    grad_slots = [score_grad] + [to_zh(score_grad, k) for k in (1, 2, 3)]
    own, other = hidden_grad_parts(index, grad_slots, head)
    other = to_core(other)
    head_grad, *parts = head_grad_parts(hidden, grad_slots)
    parts = [to_y(parts[j - 1], -j) for j in (1, 2, 3)]
    for part in parts:
        head_grad = head_grad + part.astype(f32)
    by_x = own[:2] + other[:2]
    for step in (1, 2, 3):
        part = own[2 * step : 2 * step + 2] + other[2 * step : 2 * step + 2]
        by_x = by_x + to_x(part.astype(bf16), step).astype(f32)

    def home(zl, y, zh, x, core):
        return zl, y, x % 2 * 2 + core, x // 2 * 2 + zh // 2, zh % 2

    by_zl = by_x[0] + to_zl(by_x[1])
    hidden_grad = send(by_zl.astype(bf16), home).astype(f32)
    return (kl_terms, hidden_grad, head_grad)


def solution(mesh):
    return jax.shard_map(
        step,
        mesh=mesh,
        in_specs=(
            P("dp", PLANE),
            P(PLANE),
            P(PLANE, None),
            P("dp", None),
            P("dp", PLANE),
            P("dp"),
        ),
        out_specs=(P(None, "dp"), P("dp", PLANE), P("dp", PLANE)),
        check_vma=False,
    )
```

```python
import jax
import jax.numpy as jnp
from jax import lax
from jax.experimental import pallas as pl
from jax.experimental.pallas import tpu as pltpu
from jax.sharding import PartitionSpec as P

DT = 8192
C = 4
FRAMES = 64
epsilon = 1e-05

ALL = ("group", "dp", "mp")
PLANE = ("group", "mp")


def place(zl, y, zh, x, core):
    return zl * 128 + (y % 4 * 4 + zh % 4) * 8 + x % 4 * 2 + core


def send(value, target):
    pairs = []
    for zl in range(2):
        for y in range(4):
            for zh in range(4):
                for x in range(4):
                    for core in range(2):
                        pairs.append((place(zl, y, zh, x, core), place(*target(zl, y, zh, x, core))))
    return lax.ppermute(value, ALL, pairs)


def to_y(value, step):
    return send(value, lambda zl, y, zh, x, core: (zl, y + step, zh, x, core))


def to_zh(value, step):
    return send(value, lambda zl, y, zh, x, core: (zl, y, zh + step, x, core))


def to_x(value, step):
    return send(value, lambda zl, y, zh, x, core: (zl, y, zh, x + step, core))


def to_zl(value):
    return send(value, lambda zl, y, zh, x, core: (1 - zl, y, zh, x, core))


def to_core(value):
    return send(value, lambda zl, y, zh, x, core: (zl, y, zh, x, 1 - core))


def coordinates(index):
    return index // 128, index // 32 % 4, index // 8 % 4, index // 2 % 4, index % 2


def hidden_block(k, p):
    def spot(i, index_ref):
        _, y, zh, _, core = coordinates(index_ref[0])
        return 0, (y + 8 - p - 2 * core) % 4 * 4 + (zh + k) % 4

    return pl.BlockSpec((128, 256), spot)


def pick_kernel(index_ref, *refs):
    block_refs, out_refs = refs[:6], refs[6:]
    for k in range(3):
        for p in range(2):
            out_refs[k][p] = block_refs[2 * k + p][...]


def picked_blocks(index, hidden):
    return pl.pallas_call(
        pick_kernel,
        grid_spec=pltpu.PrefetchScalarGridSpec(
            num_scalar_prefetch=1,
            grid=(1,),
            in_specs=[hidden_block(k, p) for k in (1, 2, 3) for p in range(2)],
            out_specs=[pl.BlockSpec((2, 128, 256), lambda i, index_ref: (0, 0, 0))] * 3,
        ),
        out_shape=[jax.ShapeDtypeStruct((2, 128, 256), hidden.dtype)] * 3,
        name="pick",
    )(index, *[hidden] * 6)


def split(value):
    high = value.astype(jnp.bfloat16)
    return high, (value - high.astype(jnp.float32)).astype(jnp.bfloat16)


def teacher_kernel(index_ref, hidden_ref, gain_ref, *refs):
    head_refs, out_ref, both_ref, squares_ref = refs[:4], refs[4], refs[5], refs[6]
    rows, depth = hidden_ref.shape

    @pl.when(pl.program_id(0) == 0)
    def _():
        hidden = hidden_ref[...].astype(jnp.float32)
        high, low = split(hidden * gain_ref[...].astype(jnp.float32).reshape(1, depth))
        both_ref[:rows] = high
        both_ref[rows:] = low
        eighth = jnp.full((8, depth), 0.125, jnp.bfloat16)
        squares = sum(
            lax.dot_general(eighth, part, (((1,), (1,)), ((), ())), preferred_element_type=jnp.float32)
            for part in split(hidden * hidden)
        )
        squares_ref[...] = jnp.zeros_like(squares_ref)
        squares_ref[:, :rows] = squares

    for i in range(4):
        scores = jnp.dot(both_ref[...], head_refs[i][...], preferred_element_type=jnp.float32)
        out_ref[i, :rows] = scores[:rows] + scores[rows:]
        out_ref[i, rows:] = squares_ref[...]


def teacher_parts(index, hidden, gain, head, other):
    rows, depth = hidden.shape

    def block(n):
        def spot(i, index_ref):
            zl, _, _, x, core = coordinates(index_ref[0])
            zl = (zl + n) % 2
            return 0, (zl * 4 + (x + 2 * i + n // 2) % 4) * 2 + (core + other) % 2

        return pl.BlockSpec((depth, 512), spot)

    return pl.pallas_call(
        teacher_kernel,
        grid_spec=pltpu.PrefetchScalarGridSpec(
            num_scalar_prefetch=1,
            grid=(2,),
            in_specs=[
                pl.BlockSpec((rows, depth), lambda i, index_ref: (0, 0)),
                pl.BlockSpec((depth,), lambda i, index_ref: (0,)),
                *(block(n) for n in range(4)),
            ],
            out_specs=pl.BlockSpec((4, rows + 8, 512), lambda i, index_ref: (i, 0, 0)),
            scratch_shapes=[pltpu.VMEM((2 * rows, depth), jnp.bfloat16), pltpu.VMEM((8, 512), jnp.float32)],
        ),
        out_shape=jax.ShapeDtypeStruct((8, rows + 8, 512), jnp.float32),
        name="teacher",
    )(index, hidden, gain, head, head, head, head)


def student_kernel(index_ref, *refs):
    own_refs, near_refs, far_refs, head_refs = refs[:4], refs[4:7], refs[7:10], refs[10:14]
    first_ref, out_ref, hidden_ref, head_ref = refs[14:]
    core = index_ref[0] % 2

    def spot(k, side, p):
        return pl.ds(128 * k, 128), pl.ds(pl.multiple_of((2 * side + p) * 256, 256), 256)

    for p in range(2):
        hidden_ref[spot(0, core, p)] = own_refs[p][...]
        hidden_ref[spot(0, 1 - core, p)] = own_refs[2 + p][...]
        for k in (1, 2, 3):
            hidden_ref[spot(k, core, p)] = near_refs[k - 1][p]
            hidden_ref[spot(k, 1 - core, p)] = far_refs[k - 1][p]
    for j in range(4):
        head_ref[256 * j : 256 * (j + 1)] = head_refs[j][...]
    scores = jnp.dot(hidden_ref[...], head_ref[...], preferred_element_type=jnp.float32)
    first_ref[...] = scores[:128]
    for k in (1, 2, 3):
        out_ref[k - 1] = scores[128 * k : 128 * (k + 1)]


def student_parts(index, own, near, far, head_slots):
    def whole(*shape):
        return pl.BlockSpec(shape, lambda i, index_ref: (0,) * len(shape))

    return pl.pallas_call(
        student_kernel,
        grid_spec=pltpu.PrefetchScalarGridSpec(
            num_scalar_prefetch=1,
            grid=(1,),
            in_specs=[hidden_block(0, p) for p in range(4)]
            + [whole(2, 128, 256)] * 6
            + [whole(256, 512)] * 4,
            out_specs=(whole(128, 512), whole(3, 128, 512), whole(512, 1024), whole(1024, 512)),
        ),
        out_shape=(
            jax.ShapeDtypeStruct((128, 512), jnp.float32),
            jax.ShapeDtypeStruct((3, 128, 512), jnp.float32),
            jax.ShapeDtypeStruct((512, 1024), jnp.bfloat16),
            jax.ShapeDtypeStruct((1024, 512), jnp.bfloat16),
        ),
        name="student",
    )(index, *[own] * 4, *near, *far, *head_slots)


def head_grad_kernel(hidden_ref, *refs):
    grad_refs, own_ref, out_refs, slots_ref = refs[:4], refs[4], refs[5:8], refs[8]
    for k in range(4):
        slots_ref[128 * k : 128 * (k + 1)] = grad_refs[k][...]
    for j in (1, 2, 3, 0):
        total = lax.dot_general(
            hidden_ref[:, 256 * j : 256 * (j + 1)],
            slots_ref[...],
            (((0,), (0,)), ((), ())),
            preferred_element_type=jnp.float32,
        )
        if j == 0:
            own_ref[...] = total
        else:
            out_refs[j - 1][...] = total.astype(jnp.bfloat16)


def head_grad_parts(hidden, grad_slots):
    return pl.pallas_call(
        head_grad_kernel,
        out_shape=(
            jax.ShapeDtypeStruct((256, 512), jnp.float32),
            *[jax.ShapeDtypeStruct((256, 512), jnp.bfloat16)] * 3,
        ),
        scratch_shapes=[pltpu.VMEM((512, 512), jnp.bfloat16)],
        name="head_grad",
    )(hidden, *grad_slots)


def hidden_grad_kernel(index_ref, *refs):
    grad_refs, head_ref, own_ref, other_ref, slots_ref, sorted_ref = refs[:4], *refs[4:]
    zl, y, zh, x, core = coordinates(index_ref[0])
    for k in range(4):
        slots_ref[k] = grad_refs[k][...]
    goals = [2 * m + side for side in (core, 1 - core) for m in range(2)]
    for i, goal in enumerate(goals):
        sorted_ref[128 * i : 128 * (i + 1)] = slots_ref[(zh + 4 - goal) % 4]
    for j in range(4):
        a = (y + 4 - j) % 4
        terms = lax.dot_general(
            sorted_ref[...],
            head_ref[256 * j : 256 * (j + 1)],
            (((1,), (1,)), ((), ())),
            preferred_element_type=jnp.float32,
        )
        for m in range(2):
            spot = (a % 2 * 2 + m + 4 - x) % 4 * 2 + (a // 2 + zl) % 2
            own_ref[spot] = terms[128 * m : 128 * (m + 1)]
            other_ref[spot] = terms[128 * (2 + m) : 128 * (3 + m)]


def hidden_grad_parts(index, grad_slots, head):
    return pl.pallas_call(
        hidden_grad_kernel,
        in_specs=[pl.BlockSpec(memory_space=pltpu.SMEM)] + [pl.BlockSpec(memory_space=pltpu.VMEM)] * 5,
        out_shape=(jax.ShapeDtypeStruct((8, 128, 256), jnp.float32),) * 2,
        scratch_shapes=[pltpu.VMEM((4, 128, 512), jnp.bfloat16), pltpu.VMEM((512, 512), jnp.bfloat16)],
        name="hidden_grad",
    )(index, *grad_slots, head)


def step(teacher_hidden, teacher_gain, teacher_head, student_hidden, student_head, depth_cut):
    f32, f16, bf16 = jnp.float32, jnp.float16, jnp.bfloat16
    zl = lax.axis_index("group")
    x = lax.axis_index("mp") // 2
    index = lax.axis_index(ALL).reshape(1)

    halves = picked_blocks(index, student_hidden)
    near = [to_zh(halves[k - 1], k) for k in (1, 2, 3)]
    head_slots = [student_head] + [to_y(student_head, j) for j in (1, 2, 3)]
    far = [to_core(half) for half in near]

    other = teacher_parts(index, teacher_hidden, teacher_gain, teacher_head, 1)
    other = to_core(other)
    parts = teacher_parts(index, teacher_hidden, teacher_gain, teacher_head, 0)
    by_x = parts[:2] + other[:2]
    for step in (1, 2, 3):
        part = parts[2 * step : 2 * step + 2] + other[2 * step : 2 * step + 2]
        by_x = by_x + to_x(part.astype(f16), step).astype(f32)
    teacher = by_x[0] + to_zl(by_x[1].astype(f16)).astype(f32)

    student, parts, hidden, head = student_parts(index, student_hidden, near, far, head_slots)
    parts = parts.astype(f16)
    for k in (1, 2, 3):
        student = student + to_zh(parts[k - 1], -k).astype(f32)

    row_scale = lax.rsqrt(teacher[128, :128] * (8 / DT) + epsilon)
    teacher = teacher[:128] * row_scale[:, None]

    teacher_max = jnp.max(teacher, axis=1)
    student_max = jnp.max(student, axis=1)
    teacher_exp = jnp.exp(teacher - teacher_max[:, None])
    student_exp = jnp.exp(student - student_max[:, None])
    stats = jnp.stack(
        [
            teacher_max,
            jnp.sum(teacher_exp, axis=1),
            jnp.sum(teacher_exp * (teacher - student), axis=1),
            student_max,
            jnp.sum(student_exp, axis=1),
        ]
    )
    every = jnp.stack(
        [
            stats,
            to_core(stats),
            send(stats, lambda zl, y, zh, x, core: (zl, y, zh, x ^ 1, core)),
            send(stats, lambda zl, y, zh, x, core: (zl, y, zh, x ^ 1, 1 - core)),
        ]
    )
    teacher_top = jnp.max(every[:, 0], axis=0)
    student_top = jnp.max(every[:, 3], axis=0)
    teacher_shift = jnp.exp(every[:, 0] - teacher_top)
    student_shift = jnp.exp(every[:, 3] - student_top)
    teacher_sum = jnp.sum(every[:, 1] * teacher_shift, axis=0)
    student_sum = jnp.sum(every[:, 4] * student_shift, axis=0)
    weighted = jnp.sum(every[:, 2] * teacher_shift, axis=0)
    divergence = (
        weighted / teacher_sum - (teacher_top + jnp.log(teacher_sum)) + (student_top + jnp.log(student_sum))
    )
    book = zl * 2 + x // 2
    depth_rows = jnp.repeat(depth_cut, FRAMES)
    depth_weight = (book < depth_rows).astype(f32) / depth_rows.astype(f32)
    teacher_factor = teacher_shift[0] / teacher_sum * depth_weight
    student_factor = student_shift[0] / student_sum * depth_weight
    score_grad = (
        student_exp * student_factor[:, None] - teacher_exp * teacher_factor[:, None]
    ).astype(bf16)

    own_kl = (divergence * depth_weight)[None]
    kl = [
        own_kl,
        send(own_kl, lambda zl, y, zh, x, core: (zl, y, zh, x ^ 2, core)),
        send(own_kl, lambda zl, y, zh, x, core: (1 - zl, y, zh, x, core)),
        send(own_kl, lambda zl, y, zh, x, core: (1 - zl, y, zh, x ^ 2, core)),
    ]
    kl = jnp.concatenate(kl)
    kl_terms = jnp.concatenate(
        [lax.dynamic_slice_in_dim(kl, book ^ i, 1, 0) for i in range(C)]
    )

    grad_slots = [score_grad] + [to_zh(score_grad, k) for k in (1, 2, 3)]
    own, other = hidden_grad_parts(index, grad_slots, head)
    other = to_core(other)
    head_grad, *parts = head_grad_parts(hidden, grad_slots)
    parts = [to_y(parts[j - 1], -j) for j in (1, 2, 3)]
    for part in parts:
        head_grad = head_grad + part.astype(f32)
    by_x = own[:2] + other[:2]
    for step in (1, 2, 3):
        part = own[2 * step : 2 * step + 2] + other[2 * step : 2 * step + 2]
        by_x = by_x + to_x(part.astype(bf16), step).astype(f32)

    def home(zl, y, zh, x, core):
        return zl, y, x % 2 * 2 + core, x // 2 * 2 + zh // 2, zh % 2

    by_x = by_x.astype(bf16)
    hidden_grad = send(by_x[0], home).astype(f32) + send(
        by_x[1], lambda zl, y, zh, x, core: home(1 - zl, y, zh, x, core)
    ).astype(f32)
    return (kl_terms, hidden_grad, head_grad)


def solution(mesh):
    return jax.shard_map(
        step,
        mesh=mesh,
        in_specs=(
            P("dp", PLANE),
            P(PLANE),
            P(PLANE, None),
            P("dp", None),
            P("dp", PLANE),
            P("dp"),
        ),
        out_specs=(P(None, "dp"), P("dp", PLANE), P("dp", PLANE)),
        check_vma=False,
    )
```

```python
import jax
import jax.numpy as jnp
from jax import lax
from jax.experimental import pallas as pl
from jax.experimental.pallas import tpu as pltpu
from jax.sharding import PartitionSpec as P

DT = 8192
C = 4
FRAMES = 64
epsilon = 1e-05

ALL = ("group", "dp", "mp")
PLANE = ("group", "mp")


def place(zl, y, zh, x, core):
    return zl * 128 + (y % 4 * 4 + zh % 4) * 8 + x % 4 * 2 + core


def send(value, target):
    pairs = []
    for zl in range(2):
        for y in range(4):
            for zh in range(4):
                for x in range(4):
                    for core in range(2):
                        pairs.append((place(zl, y, zh, x, core), place(*target(zl, y, zh, x, core))))
    return lax.ppermute(value, ALL, pairs)


def to_y(value, step):
    return send(value, lambda zl, y, zh, x, core: (zl, y + step, zh, x, core))


def to_zh(value, step):
    return send(value, lambda zl, y, zh, x, core: (zl, y, zh + step, x, core))


def to_x(value, step):
    return send(value, lambda zl, y, zh, x, core: (zl, y, zh, x + step, core))


def to_zl(value):
    return send(value, lambda zl, y, zh, x, core: (1 - zl, y, zh, x, core))


def round_ring(to, values, sign=1):
    received = []
    for step, value in zip((1, 2, 3), values):
        received.append(to(value, sign * step))
    return received


def to_core(value):
    return send(value, lambda zl, y, zh, x, core: (zl, y, zh, x, 1 - core))


def coordinates(index):
    return index // 128, index // 32 % 4, index // 8 % 4, index // 2 % 4, index % 2


def hidden_block(k, p):
    def spot(i, index_ref):
        _, y, zh, _, core = coordinates(index_ref[0])
        return 0, (y + 8 - p - 2 * core) % 4 * 4 + (zh + k) % 4

    return pl.BlockSpec((128, 256), spot)


def pick_kernel(index_ref, *refs):
    block_refs, out_refs = refs[:6], refs[6:]
    for k in range(3):
        for p in range(2):
            out_refs[k][p] = block_refs[2 * k + p][...]


def picked_blocks(index, hidden):
    return pl.pallas_call(
        pick_kernel,
        grid_spec=pltpu.PrefetchScalarGridSpec(
            num_scalar_prefetch=1,
            grid=(1,),
            in_specs=[hidden_block(k, p) for k in (1, 2, 3) for p in range(2)],
            out_specs=[pl.BlockSpec((2, 128, 256), lambda i, index_ref: (0, 0, 0))] * 3,
        ),
        out_shape=[jax.ShapeDtypeStruct((2, 128, 256), hidden.dtype)] * 3,
        name="pick",
    )(index, *[hidden] * 6)


def split(value):
    high = value.astype(jnp.bfloat16)
    return high, (value - high.astype(jnp.float32)).astype(jnp.bfloat16)


def teacher_kernel(index_ref, hidden_ref, gain_ref, *refs):
    head_refs, out_ref, both_ref, squares_ref = refs[:4], refs[4], refs[5], refs[6]
    rows, depth = hidden_ref.shape

    @pl.when(pl.program_id(0) == 0)
    def _():
        hidden = hidden_ref[...].astype(jnp.float32)
        high, low = split(hidden * gain_ref[...].astype(jnp.float32).reshape(1, depth))
        both_ref[:rows] = high
        both_ref[rows:] = low
        eighth = jnp.full((8, depth), 0.125, jnp.bfloat16)
        squares = sum(
            lax.dot_general(eighth, part, (((1,), (1,)), ((), ())), preferred_element_type=jnp.float32)
            for part in split(hidden * hidden)
        )
        squares_ref[...] = jnp.zeros_like(squares_ref)
        squares_ref[:, :rows] = squares

    for i in range(4):
        scores = jnp.dot(both_ref[...], head_refs[i][...], preferred_element_type=jnp.float32)
        out_ref[i, :rows] = scores[:rows] + scores[rows:]
        out_ref[i, rows:] = squares_ref[...]


def teacher_parts(index, hidden, gain, head, other):
    rows, depth = hidden.shape

    def block(n):
        def spot(i, index_ref):
            zl, _, _, x, core = coordinates(index_ref[0])
            zl = (zl + n) % 2
            return 0, (zl * 4 + (x + 2 * i + n // 2) % 4) * 2 + (core + other) % 2

        return pl.BlockSpec((depth, 512), spot)

    return pl.pallas_call(
        teacher_kernel,
        grid_spec=pltpu.PrefetchScalarGridSpec(
            num_scalar_prefetch=1,
            grid=(2,),
            in_specs=[
                pl.BlockSpec((rows, depth), lambda i, index_ref: (0, 0)),
                pl.BlockSpec((depth,), lambda i, index_ref: (0,)),
                *(block(n) for n in range(4)),
            ],
            out_specs=pl.BlockSpec((4, rows + 8, 512), lambda i, index_ref: (i, 0, 0)),
            scratch_shapes=[pltpu.VMEM((2 * rows, depth), jnp.bfloat16), pltpu.VMEM((8, 512), jnp.float32)],
        ),
        out_shape=jax.ShapeDtypeStruct((8, rows + 8, 512), jnp.float32),
        name="teacher",
    )(index, hidden, gain, head, head, head, head)


def student_kernel(index_ref, *refs):
    own_refs, near_refs, far_refs, head_refs = refs[:4], refs[4:7], refs[7:10], refs[10:14]
    first_ref, out_ref, hidden_ref, head_ref = refs[14:]
    core = index_ref[0] % 2

    def spot(k, side, p):
        return pl.ds(128 * k, 128), pl.ds(pl.multiple_of((2 * side + p) * 256, 256), 256)

    for p in range(2):
        hidden_ref[spot(0, core, p)] = own_refs[p][...]
        hidden_ref[spot(0, 1 - core, p)] = own_refs[2 + p][...]
        for k in (1, 2, 3):
            hidden_ref[spot(k, core, p)] = near_refs[k - 1][p]
            hidden_ref[spot(k, 1 - core, p)] = far_refs[k - 1][p]
    for j in range(4):
        head_ref[256 * j : 256 * (j + 1)] = head_refs[j][...]
    scores = jnp.dot(hidden_ref[...], head_ref[...], preferred_element_type=jnp.float32)
    first_ref[...] = scores[:128]
    for k in (1, 2, 3):
        out_ref[k - 1] = scores[128 * k : 128 * (k + 1)]


def student_parts(index, own, near, far, head_slots):
    def whole(*shape):
        return pl.BlockSpec(shape, lambda i, index_ref: (0,) * len(shape))

    return pl.pallas_call(
        student_kernel,
        grid_spec=pltpu.PrefetchScalarGridSpec(
            num_scalar_prefetch=1,
            grid=(1,),
            in_specs=[hidden_block(0, p) for p in range(4)]
            + [whole(2, 128, 256)] * 6
            + [whole(256, 512)] * 4,
            out_specs=(whole(128, 512), whole(3, 128, 512), whole(512, 1024), whole(1024, 512)),
        ),
        out_shape=(
            jax.ShapeDtypeStruct((128, 512), jnp.float32),
            jax.ShapeDtypeStruct((3, 128, 512), jnp.float32),
            jax.ShapeDtypeStruct((512, 1024), jnp.bfloat16),
            jax.ShapeDtypeStruct((1024, 512), jnp.bfloat16),
        ),
        name="student",
    )(index, *[own] * 4, *near, *far, *head_slots)


def head_grad_kernel(hidden_ref, *refs):
    grad_refs, own_ref, out_refs, slots_ref = refs[:4], refs[4], refs[5:8], refs[8]
    for k in range(4):
        slots_ref[128 * k : 128 * (k + 1)] = grad_refs[k][...]
    for j in (1, 2, 3, 0):
        total = lax.dot_general(
            hidden_ref[:, 256 * j : 256 * (j + 1)],
            slots_ref[...],
            (((0,), (0,)), ((), ())),
            preferred_element_type=jnp.float32,
        )
        if j == 0:
            own_ref[...] = total
        else:
            out_refs[j - 1][...] = total.astype(jnp.bfloat16)


def head_grad_parts(hidden, grad_slots):
    return pl.pallas_call(
        head_grad_kernel,
        out_shape=(
            jax.ShapeDtypeStruct((256, 512), jnp.float32),
            *[jax.ShapeDtypeStruct((256, 512), jnp.bfloat16)] * 3,
        ),
        scratch_shapes=[pltpu.VMEM((512, 512), jnp.bfloat16)],
        name="head_grad",
    )(hidden, *grad_slots)


def hidden_grad_kernel(index_ref, *refs):
    grad_refs, head_ref, own_ref, other_ref, slots_ref, sorted_ref = refs[:4], *refs[4:]
    zl, y, zh, x, core = coordinates(index_ref[0])
    for k in range(4):
        slots_ref[k] = grad_refs[k][...]
    goals = [2 * m + side for side in (core, 1 - core) for m in range(2)]
    for i, goal in enumerate(goals):
        sorted_ref[128 * i : 128 * (i + 1)] = slots_ref[(zh + 4 - goal) % 4]
    for j in range(4):
        a = (y + 4 - j) % 4
        terms = lax.dot_general(
            sorted_ref[...],
            head_ref[256 * j : 256 * (j + 1)],
            (((1,), (1,)), ((), ())),
            preferred_element_type=jnp.float32,
        )
        for m in range(2):
            spot = (a % 2 * 2 + m + 4 - x) % 4 * 2 + (a // 2 + zl) % 2
            own_ref[spot] = terms[128 * m : 128 * (m + 1)]
            other_ref[spot] = terms[128 * (2 + m) : 128 * (3 + m)]


def hidden_grad_parts(index, grad_slots, head):
    return pl.pallas_call(
        hidden_grad_kernel,
        in_specs=[pl.BlockSpec(memory_space=pltpu.SMEM)] + [pl.BlockSpec(memory_space=pltpu.VMEM)] * 5,
        out_shape=(jax.ShapeDtypeStruct((8, 128, 256), jnp.float32),) * 2,
        scratch_shapes=[pltpu.VMEM((4, 128, 512), jnp.bfloat16), pltpu.VMEM((512, 512), jnp.bfloat16)],
        name="hidden_grad",
    )(index, *grad_slots, head)


def step(teacher_hidden, teacher_gain, teacher_head, student_hidden, student_head, depth_cut):
    f32, f16, bf16 = jnp.float32, jnp.float16, jnp.bfloat16
    zl = lax.axis_index("group")
    x = lax.axis_index("mp") // 2
    index = lax.axis_index(ALL).reshape(1)

    halves = picked_blocks(index, student_hidden)
    near = round_ring(to_zh, halves)
    head_slots = [student_head, *round_ring(to_y, [student_head] * 3)]
    far = [to_core(half) for half in near]

    other = teacher_parts(index, teacher_hidden, teacher_gain, teacher_head, 1)
    other = to_core(other)
    parts = teacher_parts(index, teacher_hidden, teacher_gain, teacher_head, 0)
    by_x = parts[:2] + other[:2]
    pieces = [
        (parts[2 * step : 2 * step + 2] + other[2 * step : 2 * step + 2]).astype(f16) for step in (1, 2, 3)
    ]
    for piece in round_ring(to_x, pieces):
        by_x = by_x + piece.astype(f32)
    teacher = by_x[0] + to_zl(by_x[1].astype(f16)).astype(f32)

    student, parts, hidden, head = student_parts(index, student_hidden, near, far, head_slots)
    for part in round_ring(to_zh, parts.astype(f16), -1):
        student = student + part.astype(f32)

    row_scale = lax.rsqrt(teacher[128, :128] * (8 / DT) + epsilon)
    teacher = teacher[:128] * row_scale[:, None]

    teacher_max = jnp.max(teacher, axis=1)
    student_max = jnp.max(student, axis=1)
    teacher_exp = jnp.exp(teacher - teacher_max[:, None])
    student_exp = jnp.exp(student - student_max[:, None])
    stats = jnp.stack(
        [
            teacher_max,
            jnp.sum(teacher_exp, axis=1),
            jnp.sum(teacher_exp * (teacher - student), axis=1),
            student_max,
            jnp.sum(student_exp, axis=1),
        ]
    )
    every = jnp.stack(
        [
            stats,
            to_core(stats),
            send(stats, lambda zl, y, zh, x, core: (zl, y, zh, x ^ 1, core)),
            send(stats, lambda zl, y, zh, x, core: (zl, y, zh, x ^ 1, 1 - core)),
        ]
    )
    teacher_top = jnp.max(every[:, 0], axis=0)
    student_top = jnp.max(every[:, 3], axis=0)
    teacher_shift = jnp.exp(every[:, 0] - teacher_top)
    student_shift = jnp.exp(every[:, 3] - student_top)
    teacher_sum = jnp.sum(every[:, 1] * teacher_shift, axis=0)
    student_sum = jnp.sum(every[:, 4] * student_shift, axis=0)
    weighted = jnp.sum(every[:, 2] * teacher_shift, axis=0)
    divergence = (
        weighted / teacher_sum - (teacher_top + jnp.log(teacher_sum)) + (student_top + jnp.log(student_sum))
    )
    book = zl * 2 + x // 2
    depth_rows = jnp.repeat(depth_cut, FRAMES)
    depth_weight = (book < depth_rows).astype(f32) / depth_rows.astype(f32)
    teacher_factor = teacher_shift[0] / teacher_sum * depth_weight
    student_factor = student_shift[0] / student_sum * depth_weight
    score_grad = (
        student_exp * student_factor[:, None] - teacher_exp * teacher_factor[:, None]
    ).astype(bf16)

    own_kl = (divergence * depth_weight)[None]
    kl = [
        own_kl,
        send(own_kl, lambda zl, y, zh, x, core: (zl, y, zh, x ^ 2, core)),
        send(own_kl, lambda zl, y, zh, x, core: (1 - zl, y, zh, x, core)),
        send(own_kl, lambda zl, y, zh, x, core: (1 - zl, y, zh, x ^ 2, core)),
    ]
    kl = jnp.concatenate(kl)
    kl_terms = jnp.concatenate(
        [lax.dynamic_slice_in_dim(kl, book ^ i, 1, 0) for i in range(C)]
    )

    grad_slots = [score_grad, *round_ring(to_zh, [score_grad] * 3)]
    own, other = hidden_grad_parts(index, grad_slots, head)
    other = to_core(other)
    head_grad, *parts = head_grad_parts(hidden, grad_slots)
    parts = round_ring(to_y, parts, -1)
    for part in parts:
        head_grad = head_grad + part.astype(f32)
    by_x = own[:2] + other[:2]
    pieces = [
        (own[2 * step : 2 * step + 2] + other[2 * step : 2 * step + 2]).astype(bf16) for step in (1, 2, 3)
    ]
    for piece in round_ring(to_x, pieces):
        by_x = by_x + piece.astype(f32)

    def home(zl, y, zh, x, core):
        return zl, y, x % 2 * 2 + core, x // 2 * 2 + zh // 2, zh % 2

    by_x = by_x.astype(bf16)
    hidden_grad = send(by_x[0], home).astype(f32) + send(
        by_x[1], lambda zl, y, zh, x, core: home(1 - zl, y, zh, x, core)
    ).astype(f32)
    return (kl_terms, hidden_grad, head_grad)


def solution(mesh):
    return jax.shard_map(
        step,
        mesh=mesh,
        in_specs=(
            P("dp", PLANE),
            P(PLANE),
            P(PLANE, None),
            P("dp", None),
            P("dp", PLANE),
            P("dp"),
        ),
        out_specs=(P(None, "dp"), P("dp", PLANE), P("dp", PLANE)),
        check_vma=False,
    )
```

```python
import jax
import jax.numpy as jnp
from jax import lax
from jax.experimental import pallas as pl
from jax.experimental.pallas import tpu as pltpu
from jax.sharding import PartitionSpec as P

DT = 8192
C = 4
FRAMES = 64
epsilon = 1e-05

ALL = ("group", "dp", "mp")
PLANE = ("group", "mp")


def place(zl, y, zh, x, core):
    return zl * 128 + (y % 4 * 4 + zh % 4) * 8 + x % 4 * 2 + core


def send(value, target):
    pairs = []
    for zl in range(2):
        for y in range(4):
            for zh in range(4):
                for x in range(4):
                    for core in range(2):
                        pairs.append((place(zl, y, zh, x, core), place(*target(zl, y, zh, x, core))))
    return lax.ppermute(value, ALL, pairs)


def to_y(value, step):
    return send(value, lambda zl, y, zh, x, core: (zl, y + step, zh, x, core))


def to_zh(value, step):
    return send(value, lambda zl, y, zh, x, core: (zl, y, zh + step, x, core))


def to_x(value, step):
    return send(value, lambda zl, y, zh, x, core: (zl, y, zh, x + step, core))


def to_zl(value):
    return send(value, lambda zl, y, zh, x, core: (1 - zl, y, zh, x, core))


def round_ring(to, values, sign=1):
    received = []
    for step, value in zip((1, 2, 3), values):
        received.append(to(value, sign * step))
    return received


def to_core(value):
    return send(value, lambda zl, y, zh, x, core: (zl, y, zh, x, 1 - core))


def coordinates(index):
    return index // 128, index // 32 % 4, index // 8 % 4, index // 2 % 4, index % 2


def hidden_block(k, p):
    def spot(i, index_ref):
        _, y, zh, _, core = coordinates(index_ref[0])
        return 0, (y + 8 - p - 2 * core) % 4 * 4 + (zh + k) % 4

    return pl.BlockSpec((128, 256), spot)


def pick_kernel(index_ref, *refs):
    block_refs, out_refs = refs[:6], refs[6:]
    for k in range(3):
        for p in range(2):
            out_refs[k][p] = block_refs[2 * k + p][...]


def picked_blocks(index, hidden):
    return pl.pallas_call(
        pick_kernel,
        grid_spec=pltpu.PrefetchScalarGridSpec(
            num_scalar_prefetch=1,
            grid=(1,),
            in_specs=[hidden_block(k, p) for k in (1, 2, 3) for p in range(2)],
            out_specs=[pl.BlockSpec((2, 128, 256), lambda i, index_ref: (0, 0, 0))] * 3,
        ),
        out_shape=[jax.ShapeDtypeStruct((2, 128, 256), hidden.dtype)] * 3,
        name="pick",
    )(index, *[hidden] * 6)


def split(value):
    high = value.astype(jnp.bfloat16)
    return high, (value - high.astype(jnp.float32)).astype(jnp.bfloat16)


def teacher_kernel(index_ref, hidden_ref, gain_ref, *refs):
    head_refs, out_ref, both_ref, squares_ref = refs[:4], refs[4], refs[5], refs[6]
    rows, depth = hidden_ref.shape

    @pl.when(pl.program_id(0) == 0)
    def _():
        hidden = hidden_ref[...].astype(jnp.float32)
        high, low = split(hidden * gain_ref[...].astype(jnp.float32).reshape(1, depth))
        both_ref[:rows] = high
        both_ref[rows:] = low
        eighth = jnp.full((8, depth), 0.125, jnp.bfloat16)
        squares = sum(
            lax.dot_general(eighth, part, (((1,), (1,)), ((), ())), preferred_element_type=jnp.float32)
            for part in split(hidden * hidden)
        )
        squares_ref[...] = jnp.zeros_like(squares_ref)
        squares_ref[:, :rows] = squares

    for i in range(4):
        scores = jnp.dot(both_ref[...], head_refs[i][...], preferred_element_type=jnp.float32)
        out_ref[i, :rows] = scores[:rows] + scores[rows:]
        out_ref[i, rows:] = squares_ref[...]


def teacher_parts(index, hidden, gain, head, other):
    rows, depth = hidden.shape

    def block(n):
        def spot(i, index_ref):
            zl, _, _, x, core = coordinates(index_ref[0])
            zl = (zl + n) % 2
            return 0, (zl * 4 + (x + 2 * i + n // 2) % 4) * 2 + (core + other) % 2

        return pl.BlockSpec((depth, 512), spot)

    return pl.pallas_call(
        teacher_kernel,
        grid_spec=pltpu.PrefetchScalarGridSpec(
            num_scalar_prefetch=1,
            grid=(2,),
            in_specs=[
                pl.BlockSpec((rows, depth), lambda i, index_ref: (0, 0)),
                pl.BlockSpec((depth,), lambda i, index_ref: (0,)),
                *(block(n) for n in range(4)),
            ],
            out_specs=pl.BlockSpec((4, rows + 8, 512), lambda i, index_ref: (i, 0, 0)),
            scratch_shapes=[pltpu.VMEM((2 * rows, depth), jnp.bfloat16), pltpu.VMEM((8, 512), jnp.float32)],
        ),
        out_shape=jax.ShapeDtypeStruct((8, rows + 8, 512), jnp.float32),
        name="teacher",
    )(index, hidden, gain, head, head, head, head)


def student_kernel(index_ref, *refs):
    own_refs, near_refs, far_refs, head_refs = refs[:4], refs[4:7], refs[7:10], refs[10:14]
    first_ref, out_ref, hidden_ref, head_ref = refs[14:]
    core = index_ref[0] % 2

    def spot(k, side, p):
        return pl.ds(128 * k, 128), pl.ds(pl.multiple_of((2 * side + p) * 256, 256), 256)

    for p in range(2):
        hidden_ref[spot(0, core, p)] = own_refs[p][...]
        hidden_ref[spot(0, 1 - core, p)] = own_refs[2 + p][...]
        for k in (1, 2, 3):
            hidden_ref[spot(k, core, p)] = near_refs[k - 1][p]
            hidden_ref[spot(k, 1 - core, p)] = far_refs[k - 1][p]
    for j in range(4):
        head_ref[256 * j : 256 * (j + 1)] = head_refs[j][...]
    scores = jnp.dot(hidden_ref[...], head_ref[...], preferred_element_type=jnp.float32)
    first_ref[...] = scores[:128]
    for k in (1, 2, 3):
        out_ref[k - 1] = scores[128 * k : 128 * (k + 1)]


def student_parts(index, own, near, far, head_slots):
    def whole(*shape):
        return pl.BlockSpec(shape, lambda i, index_ref: (0,) * len(shape))

    return pl.pallas_call(
        student_kernel,
        grid_spec=pltpu.PrefetchScalarGridSpec(
            num_scalar_prefetch=1,
            grid=(1,),
            in_specs=[hidden_block(0, p) for p in range(4)]
            + [whole(2, 128, 256)] * 6
            + [whole(256, 512)] * 4,
            out_specs=(whole(128, 512), whole(3, 128, 512), whole(512, 1024), whole(1024, 512)),
        ),
        out_shape=(
            jax.ShapeDtypeStruct((128, 512), jnp.float32),
            jax.ShapeDtypeStruct((3, 128, 512), jnp.float32),
            jax.ShapeDtypeStruct((512, 1024), jnp.bfloat16),
            jax.ShapeDtypeStruct((1024, 512), jnp.bfloat16),
        ),
        name="student",
    )(index, *[own] * 4, *near, *far, *head_slots)


def head_grad_kernel(hidden_ref, *refs):
    grad_refs, own_ref, out_refs, slots_ref = refs[:4], refs[4], refs[5:8], refs[8]
    for k in range(4):
        slots_ref[128 * k : 128 * (k + 1)] = grad_refs[k][...]
    for j in (1, 2, 3, 0):
        total = lax.dot_general(
            hidden_ref[:, 256 * j : 256 * (j + 1)],
            slots_ref[...],
            (((0,), (0,)), ((), ())),
            preferred_element_type=jnp.float32,
        )
        if j == 0:
            own_ref[...] = total
        else:
            out_refs[j - 1][...] = total.astype(jnp.bfloat16)


def head_grad_parts(hidden, grad_slots):
    return pl.pallas_call(
        head_grad_kernel,
        out_shape=(
            jax.ShapeDtypeStruct((256, 512), jnp.float32),
            *[jax.ShapeDtypeStruct((256, 512), jnp.bfloat16)] * 3,
        ),
        scratch_shapes=[pltpu.VMEM((512, 512), jnp.bfloat16)],
        name="head_grad",
    )(hidden, *grad_slots)


def hidden_grad_kernel(index_ref, *refs):
    grad_refs, head_ref, own_ref, other_ref, slots_ref, sorted_ref = refs[:4], *refs[4:]
    zl, y, zh, x, core = coordinates(index_ref[0])
    for k in range(4):
        slots_ref[k] = grad_refs[k][...]
    goals = [2 * m + side for side in (core, 1 - core) for m in range(2)]
    for i, goal in enumerate(goals):
        sorted_ref[128 * i : 128 * (i + 1)] = slots_ref[(zh + 4 - goal) % 4]
    for j in range(4):
        a = (y + 4 - j) % 4
        terms = lax.dot_general(
            sorted_ref[...],
            head_ref[256 * j : 256 * (j + 1)],
            (((1,), (1,)), ((), ())),
            preferred_element_type=jnp.float32,
        )
        for m in range(2):
            spot = (a % 2 * 2 + m + 4 - x) % 4 * 2 + (a // 2 + zl) % 2
            own_ref[spot] = terms[128 * m : 128 * (m + 1)]
            other_ref[spot] = terms[128 * (2 + m) : 128 * (3 + m)]


def hidden_grad_parts(index, grad_slots, head):
    return pl.pallas_call(
        hidden_grad_kernel,
        in_specs=[pl.BlockSpec(memory_space=pltpu.SMEM)] + [pl.BlockSpec(memory_space=pltpu.VMEM)] * 5,
        out_shape=(jax.ShapeDtypeStruct((8, 128, 256), jnp.float32),) * 2,
        scratch_shapes=[pltpu.VMEM((4, 128, 512), jnp.bfloat16), pltpu.VMEM((512, 512), jnp.bfloat16)],
        name="hidden_grad",
    )(index, *grad_slots, head)


def step(teacher_hidden, teacher_gain, teacher_head, student_hidden, student_head, depth_cut):
    f32, f16, bf16 = jnp.float32, jnp.float16, jnp.bfloat16
    zl = lax.axis_index("group")
    x = lax.axis_index("mp") // 2
    index = lax.axis_index(ALL).reshape(1)

    halves = picked_blocks(index, student_hidden)
    near = round_ring(to_zh, halves)
    head_slots = [student_head, *round_ring(to_y, [student_head] * 3)]
    far = [to_core(half) for half in near]

    other = teacher_parts(index, teacher_hidden, teacher_gain, teacher_head, 1)
    other = to_core(other)
    parts = teacher_parts(index, teacher_hidden, teacher_gain, teacher_head, 0)
    by_x = parts[:2] + other[:2]
    pieces = [
        (parts[2 * step : 2 * step + 2] + other[2 * step : 2 * step + 2]).astype(f16) for step in (1, 2, 3)
    ]
    for piece in round_ring(to_x, pieces):
        by_x = by_x + piece.astype(f32)
    teacher = by_x[0] + to_zl(by_x[1].astype(f16)).astype(f32)

    student, parts, hidden, head = student_parts(index, student_hidden, near, far, head_slots)
    for part in round_ring(to_zh, parts.astype(f16), -1):
        student = student + part.astype(f32)

    row_scale = lax.rsqrt(teacher[128, :128] * (8 / DT) + epsilon)
    teacher = teacher[:128] * row_scale[:, None]

    teacher_max = jnp.max(teacher, axis=1)
    student_max = jnp.max(student, axis=1)
    teacher_exp = jnp.exp(teacher - teacher_max[:, None])
    student_exp = jnp.exp(student - student_max[:, None])
    stats = jnp.stack(
        [
            teacher_max,
            jnp.sum(teacher_exp, axis=1),
            jnp.sum(teacher_exp * (teacher - student), axis=1),
            student_max,
            jnp.sum(student_exp, axis=1),
        ]
    )
    every = jnp.stack(
        [
            stats,
            to_core(stats),
            send(stats, lambda zl, y, zh, x, core: (zl, y, zh, x ^ 1, core)),
            send(stats, lambda zl, y, zh, x, core: (zl, y, zh, x ^ 1, 1 - core)),
        ]
    )
    teacher_top = jnp.max(every[:, 0], axis=0)
    student_top = jnp.max(every[:, 3], axis=0)
    teacher_shift = jnp.exp(every[:, 0] - teacher_top)
    student_shift = jnp.exp(every[:, 3] - student_top)
    teacher_sum = jnp.sum(every[:, 1] * teacher_shift, axis=0)
    student_sum = jnp.sum(every[:, 4] * student_shift, axis=0)
    weighted = jnp.sum(every[:, 2] * teacher_shift, axis=0)
    divergence = (
        weighted / teacher_sum - (teacher_top + jnp.log(teacher_sum)) + (student_top + jnp.log(student_sum))
    )
    book = zl * 2 + x // 2
    depth_rows = jnp.repeat(depth_cut, FRAMES)
    depth_weight = (book < depth_rows).astype(f32) / depth_rows.astype(f32)
    teacher_factor = teacher_shift[0] / teacher_sum * depth_weight
    student_factor = student_shift[0] / student_sum * depth_weight
    score_grad = (
        student_exp * student_factor[:, None] - teacher_exp * teacher_factor[:, None]
    ).astype(bf16)

    own_kl = (divergence * depth_weight)[None]
    kl = [
        own_kl,
        send(own_kl, lambda zl, y, zh, x, core: (zl, y, zh, x ^ 2, core)),
        send(own_kl, lambda zl, y, zh, x, core: (1 - zl, y, zh, x, core)),
        send(own_kl, lambda zl, y, zh, x, core: (1 - zl, y, zh, x ^ 2, core)),
    ]
    kl = jnp.concatenate(kl)
    kl_terms = jnp.concatenate(
        [lax.dynamic_slice_in_dim(kl, book ^ i, 1, 0) for i in range(C)]
    )

    grad_slots = [score_grad, *round_ring(to_zh, [score_grad] * 3)]
    own, other = hidden_grad_parts(index, grad_slots, head)
    other = to_core(other)
    head_grad, *parts = head_grad_parts(hidden, grad_slots)
    parts = round_ring(to_y, parts, -1)
    for part in parts:
        head_grad = head_grad + part.astype(f32)
    pieces = [own[i] + other[i] for i in range(8)]
    hidden_grad = pieces[0]
    for piece in round_ring(to_x, [pieces[i].astype(bf16) for i in (2, 4, 6)]):
        hidden_grad = hidden_grad + piece.astype(f32)
    for step in (2, 1, 3, 0):
        piece = send(
            pieces[2 * step + 1].astype(bf16),
            lambda zl, y, zh, x, core: (1 - zl, y, zh, x + step, core),
        )
        hidden_grad = hidden_grad + piece.astype(f32)

    def home(zl, y, zh, x, core):
        return zl, y, x % 2 * 2 + core, x // 2 * 2 + zh // 2, zh % 2

    hidden_grad = send(hidden_grad.astype(bf16), home).astype(f32)
    return (kl_terms, hidden_grad, head_grad)


def solution(mesh):
    return jax.shard_map(
        step,
        mesh=mesh,
        in_specs=(
            P("dp", PLANE),
            P(PLANE),
            P(PLANE, None),
            P("dp", None),
            P("dp", PLANE),
            P("dp"),
        ),
        out_specs=(P(None, "dp"), P("dp", PLANE), P("dp", PLANE)),
        check_vma=False,
    )
```

```python
import jax
import jax.numpy as jnp
from jax import lax
from jax.experimental import pallas as pl
from jax.experimental.pallas import tpu as pltpu
from jax.sharding import PartitionSpec as P

DT = 8192
C = 4
FRAMES = 64
epsilon = 1e-05

ALL = ("group", "dp", "mp")
PLANE = ("group", "mp")


def place(zl, y, zh, x, core):
    return zl * 128 + (y % 4 * 4 + zh % 4) * 8 + x % 4 * 2 + core


def send(value, target):
    pairs = []
    for zl in range(2):
        for y in range(4):
            for zh in range(4):
                for x in range(4):
                    for core in range(2):
                        pairs.append((place(zl, y, zh, x, core), place(*target(zl, y, zh, x, core))))
    return lax.ppermute(value, ALL, pairs)


def to_y(value, step):
    return send(value, lambda zl, y, zh, x, core: (zl, y + step, zh, x, core))


def to_zh(value, step):
    return send(value, lambda zl, y, zh, x, core: (zl, y, zh + step, x, core))


def to_x(value, step):
    return send(value, lambda zl, y, zh, x, core: (zl, y, zh, x + step, core))


def to_zl(value):
    return send(value, lambda zl, y, zh, x, core: (1 - zl, y, zh, x, core))


def round_ring(to, values, sign=1):
    received = []
    for step, value in zip((1, 2, 3), values):
        received.append(to(value, sign * step))
    return received


def to_core(value):
    return send(value, lambda zl, y, zh, x, core: (zl, y, zh, x, 1 - core))


def coordinates(index):
    return index // 128, index // 32 % 4, index // 8 % 4, index // 2 % 4, index % 2


def hidden_block(k, p):
    def spot(i, index_ref):
        _, y, zh, _, core = coordinates(index_ref[0])
        return 0, (y + 8 - p - 2 * core) % 4 * 4 + (zh + k) % 4

    return pl.BlockSpec((128, 256), spot)


def pick_kernel(index_ref, *refs):
    block_refs, out_refs = refs[:6], refs[6:]
    for k in range(3):
        for p in range(2):
            out_refs[k][p] = block_refs[2 * k + p][...]


def picked_blocks(index, hidden):
    return pl.pallas_call(
        pick_kernel,
        grid_spec=pltpu.PrefetchScalarGridSpec(
            num_scalar_prefetch=1,
            grid=(1,),
            in_specs=[hidden_block(k, p) for k in (1, 2, 3) for p in range(2)],
            out_specs=[pl.BlockSpec((2, 128, 256), lambda i, index_ref: (0, 0, 0))] * 3,
        ),
        out_shape=[jax.ShapeDtypeStruct((2, 128, 256), hidden.dtype)] * 3,
        name="pick",
    )(index, *[hidden] * 6)


def split(value):
    high = value.astype(jnp.bfloat16)
    return high, (value - high.astype(jnp.float32)).astype(jnp.bfloat16)


def teacher_kernel(index_ref, hidden_ref, gain_ref, *refs):
    head_refs, out_ref, both_ref, squares_ref = refs[:4], refs[4], refs[5], refs[6]
    rows, depth = hidden_ref.shape

    @pl.when(pl.program_id(0) == 0)
    def _():
        hidden = hidden_ref[...].astype(jnp.float32)
        high, low = split(hidden * gain_ref[...].astype(jnp.float32).reshape(1, depth))
        both_ref[:rows] = high
        both_ref[rows:] = low
        eighth = jnp.full((8, depth), 0.125, jnp.bfloat16)
        squares = sum(
            lax.dot_general(eighth, part, (((1,), (1,)), ((), ())), preferred_element_type=jnp.float32)
            for part in split(hidden * hidden)
        )
        squares_ref[...] = jnp.zeros_like(squares_ref)
        squares_ref[:, :rows] = squares

    for i in range(4):
        scores = jnp.dot(both_ref[...], head_refs[i][...], preferred_element_type=jnp.float32)
        out_ref[i, :rows] = scores[:rows] + scores[rows:]
        out_ref[i, rows:] = squares_ref[...]


def teacher_parts(index, hidden, gain, head, other):
    rows, depth = hidden.shape

    def block(n):
        def spot(i, index_ref):
            zl, _, _, x, core = coordinates(index_ref[0])
            zl = (zl + n) % 2
            return 0, (zl * 4 + (x + 2 * i + n // 2) % 4) * 2 + (core + other) % 2

        return pl.BlockSpec((depth, 512), spot)

    return pl.pallas_call(
        teacher_kernel,
        grid_spec=pltpu.PrefetchScalarGridSpec(
            num_scalar_prefetch=1,
            grid=(2,),
            in_specs=[
                pl.BlockSpec((rows, depth), lambda i, index_ref: (0, 0)),
                pl.BlockSpec((depth,), lambda i, index_ref: (0,)),
                *(block(n) for n in range(4)),
            ],
            out_specs=pl.BlockSpec((4, rows + 8, 512), lambda i, index_ref: (i, 0, 0)),
            scratch_shapes=[pltpu.VMEM((2 * rows, depth), jnp.bfloat16), pltpu.VMEM((8, 512), jnp.float32)],
        ),
        out_shape=jax.ShapeDtypeStruct((8, rows + 8, 512), jnp.float32),
        name="teacher",
    )(index, hidden, gain, head, head, head, head)


def student_kernel(index_ref, *refs):
    own_refs, near_refs, far_refs, head_refs = refs[:4], refs[4:7], refs[7:10], refs[10:14]
    first_ref, out_ref, hidden_ref, head_ref = refs[14:]
    core = index_ref[0] % 2

    def spot(k, side, p):
        return pl.ds(128 * k, 128), pl.ds(pl.multiple_of((2 * side + p) * 256, 256), 256)

    for p in range(2):
        hidden_ref[spot(0, core, p)] = own_refs[p][...]
        hidden_ref[spot(0, 1 - core, p)] = own_refs[2 + p][...]
        for k in (1, 2, 3):
            hidden_ref[spot(k, core, p)] = near_refs[k - 1][p]
            hidden_ref[spot(k, 1 - core, p)] = far_refs[k - 1][p]
    for j in range(4):
        head_ref[256 * j : 256 * (j + 1)] = head_refs[j][...]
    scores = jnp.dot(hidden_ref[...], head_ref[...], preferred_element_type=jnp.float32)
    first_ref[...] = scores[:128]
    for k in (1, 2, 3):
        out_ref[k - 1] = scores[128 * k : 128 * (k + 1)]


def student_parts(index, own, near, far, head_slots):
    def whole(*shape):
        return pl.BlockSpec(shape, lambda i, index_ref: (0,) * len(shape))

    return pl.pallas_call(
        student_kernel,
        grid_spec=pltpu.PrefetchScalarGridSpec(
            num_scalar_prefetch=1,
            grid=(1,),
            in_specs=[hidden_block(0, p) for p in range(4)]
            + [whole(2, 128, 256)] * 6
            + [whole(256, 512)] * 4,
            out_specs=(whole(128, 512), whole(3, 128, 512), whole(512, 1024), whole(1024, 512)),
        ),
        out_shape=(
            jax.ShapeDtypeStruct((128, 512), jnp.float32),
            jax.ShapeDtypeStruct((3, 128, 512), jnp.float32),
            jax.ShapeDtypeStruct((512, 1024), jnp.bfloat16),
            jax.ShapeDtypeStruct((1024, 512), jnp.bfloat16),
        ),
        name="student",
    )(index, *[own] * 4, *near, *far, *head_slots)


def head_grad_kernel(hidden_ref, *refs):
    grad_refs, own_ref, out_refs, slots_ref = refs[:4], refs[4], refs[5:8], refs[8]
    for k in range(4):
        slots_ref[128 * k : 128 * (k + 1)] = grad_refs[k][...]
    for j in (1, 2, 3, 0):
        total = lax.dot_general(
            hidden_ref[:, 256 * j : 256 * (j + 1)],
            slots_ref[...],
            (((0,), (0,)), ((), ())),
            preferred_element_type=jnp.float32,
        )
        if j == 0:
            own_ref[...] = total
        else:
            out_refs[j - 1][...] = total.astype(jnp.bfloat16)


def head_grad_parts(hidden, grad_slots):
    return pl.pallas_call(
        head_grad_kernel,
        out_shape=(
            jax.ShapeDtypeStruct((256, 512), jnp.float32),
            *[jax.ShapeDtypeStruct((256, 512), jnp.bfloat16)] * 3,
        ),
        scratch_shapes=[pltpu.VMEM((512, 512), jnp.bfloat16)],
        name="head_grad",
    )(hidden, *grad_slots)


def hidden_grad_kernel(index_ref, *refs):
    grad_refs, head_ref, own_ref, other_ref, slots_ref, sorted_ref = refs[:4], *refs[4:]
    zl, y, zh, x, core = coordinates(index_ref[0])
    for k in range(4):
        slots_ref[k] = grad_refs[k][...]
    goals = [2 * m + side for side in (core, 1 - core) for m in range(2)]
    for i, goal in enumerate(goals):
        sorted_ref[128 * i : 128 * (i + 1)] = slots_ref[(zh + 4 - goal) % 4]
    for j in range(4):
        a = (y + 4 - j) % 4
        terms = lax.dot_general(
            sorted_ref[...],
            head_ref[256 * j : 256 * (j + 1)],
            (((1,), (1,)), ((), ())),
            preferred_element_type=jnp.float32,
        )
        for m in range(2):
            spot = (a % 2 * 2 + m + 4 - x) % 4 * 2 + (a // 2 + zl) % 2
            own_ref[spot] = terms[128 * m : 128 * (m + 1)]
            other_ref[spot] = terms[128 * (2 + m) : 128 * (3 + m)]


def hidden_grad_parts(index, grad_slots, head):
    return pl.pallas_call(
        hidden_grad_kernel,
        in_specs=[pl.BlockSpec(memory_space=pltpu.SMEM)] + [pl.BlockSpec(memory_space=pltpu.VMEM)] * 5,
        out_shape=(jax.ShapeDtypeStruct((8, 128, 256), jnp.float32),) * 2,
        scratch_shapes=[pltpu.VMEM((4, 128, 512), jnp.bfloat16), pltpu.VMEM((512, 512), jnp.bfloat16)],
        name="hidden_grad",
    )(index, *grad_slots, head)


def step(teacher_hidden, teacher_gain, teacher_head, student_hidden, student_head, depth_cut):
    f32, f16, bf16 = jnp.float32, jnp.float16, jnp.bfloat16
    zl = lax.axis_index("group")
    x = lax.axis_index("mp") // 2
    index = lax.axis_index(ALL).reshape(1)

    halves = picked_blocks(index, student_hidden)
    near = round_ring(to_zh, halves)
    head_slots = [student_head, *round_ring(to_y, [student_head] * 3)]
    far = [to_core(half) for half in near]

    other = teacher_parts(index, teacher_hidden, teacher_gain, teacher_head, 1)
    other = to_core(other)
    parts = teacher_parts(index, teacher_hidden, teacher_gain, teacher_head, 0)
    by_x = parts[:2] + other[:2]
    pieces = [
        (parts[2 * step : 2 * step + 2] + other[2 * step : 2 * step + 2]).astype(f16) for step in (1, 2, 3)
    ]
    for piece in round_ring(to_x, pieces):
        by_x = by_x + piece.astype(f32)
    teacher = by_x[0] + to_zl(by_x[1].astype(f16)).astype(f32)

    student, parts, hidden, head = student_parts(index, student_hidden, near, far, head_slots)
    for part in round_ring(to_zh, parts.astype(f16), -1):
        student = student + part.astype(f32)

    row_scale = lax.rsqrt(teacher[128, :128] * (8 / DT) + epsilon)
    teacher = teacher[:128] * row_scale[:, None]

    teacher_max = jnp.max(teacher, axis=1)
    student_max = jnp.max(student, axis=1)
    teacher_exp = jnp.exp(teacher - teacher_max[:, None])
    student_exp = jnp.exp(student - student_max[:, None])
    stats = jnp.stack(
        [
            teacher_max,
            jnp.sum(teacher_exp, axis=1),
            jnp.sum(teacher_exp * (teacher - student), axis=1),
            student_max,
            jnp.sum(student_exp, axis=1),
        ]
    )
    every = jnp.stack(
        [
            stats,
            to_core(stats),
            send(stats, lambda zl, y, zh, x, core: (zl, y, zh, x ^ 1, core)),
            send(stats, lambda zl, y, zh, x, core: (zl, y, zh, x ^ 1, 1 - core)),
        ]
    )
    teacher_top = jnp.max(every[:, 0], axis=0)
    student_top = jnp.max(every[:, 3], axis=0)
    teacher_shift = jnp.exp(every[:, 0] - teacher_top)
    student_shift = jnp.exp(every[:, 3] - student_top)
    teacher_sum = jnp.sum(every[:, 1] * teacher_shift, axis=0)
    student_sum = jnp.sum(every[:, 4] * student_shift, axis=0)
    weighted = jnp.sum(every[:, 2] * teacher_shift, axis=0)
    divergence = (
        weighted / teacher_sum - (teacher_top + jnp.log(teacher_sum)) + (student_top + jnp.log(student_sum))
    )
    book = zl * 2 + x // 2
    depth_rows = jnp.repeat(depth_cut, FRAMES)
    depth_weight = (book < depth_rows).astype(f32) / depth_rows.astype(f32)
    teacher_factor = teacher_shift[0] / teacher_sum * depth_weight
    student_factor = student_shift[0] / student_sum * depth_weight
    score_grad = (
        student_exp * student_factor[:, None] - teacher_exp * teacher_factor[:, None]
    ).astype(bf16)

    own_kl = (divergence * depth_weight)[None]
    kl = [
        own_kl,
        send(own_kl, lambda zl, y, zh, x, core: (zl, y, zh, x ^ 2, core)),
        send(own_kl, lambda zl, y, zh, x, core: (1 - zl, y, zh, x, core)),
        send(own_kl, lambda zl, y, zh, x, core: (1 - zl, y, zh, x ^ 2, core)),
    ]
    kl = jnp.concatenate(kl)
    kl_terms = jnp.concatenate(
        [lax.dynamic_slice_in_dim(kl, book ^ i, 1, 0) for i in range(C)]
    )

    grad_slots = [score_grad, *round_ring(to_zh, [score_grad] * 3)]
    own, other = hidden_grad_parts(index, grad_slots, head)
    other = to_core(other)
    head_grad, *parts = head_grad_parts(hidden, grad_slots)
    parts = round_ring(to_y, parts, -1)
    for part in parts:
        head_grad = head_grad + part.astype(f32)
    by_x = own[:2] + other[:2]
    pieces = [
        (own[2 * step : 2 * step + 2] + other[2 * step : 2 * step + 2]).astype(bf16) for step in (1, 2, 3)
    ]
    for piece in round_ring(to_x, pieces):
        by_x = by_x + piece.astype(f32)

    def home(zl, y, zh, x, core):
        return zl, y, x % 2 * 2 + core, x // 2 * 2 + zh // 2, zh % 2

    by_x = by_x.astype(bf16)
    same = send(by_x[0], home)
    other = send(by_x[1], lambda zl, y, zh, x, core: home(1 - zl, y, zh, x, core))
    hidden_grad = same.astype(f32) + other.astype(f32)
    return (kl_terms, hidden_grad, head_grad)


def solution(mesh):
    return jax.shard_map(
        step,
        mesh=mesh,
        in_specs=(
            P("dp", PLANE),
            P(PLANE),
            P(PLANE, None),
            P("dp", None),
            P("dp", PLANE),
            P("dp"),
        ),
        out_specs=(P(None, "dp"), P("dp", PLANE), P("dp", PLANE)),
        check_vma=False,
    )
```
